32 devices in a mesh: blk: 8 (over z, x), grp: 4 (over y, core).
Axes of the slice: x: 2, y: 2, z: 4, core: 2. Of those that a mesh axis runs over, the one named last changes fastest.
Arguments:
- flow: float32 [384, 5, 4096], P(('blk', 'grp')), may hold values from -3 to 6, as said below
- adjoint: float32 [384, 5, 4096], P(('blk', 'grp')), may hold values from -6 to 6
- cut_flag: int32 [384, 4096], P(('blk', 'grp')), may hold values 0 or 1
- lateral_owner: int32 [384, 4, 1], P(('blk', 'grp')), may hold values from 0 to 7; in each aligned block of 48 rows (0 to 47, 48 to 95, ..., all dimensions but the last counted through in order) at most 9 rows name the same one
- lateral_link: int32 [384, 4], P(('blk', 'grp')), may hold values from 0 to 59
- vertical_link: int32 [384, 2], P(('blk', 'grp')), may hold values from 0 to 59
Outputs:
- indicator: float32 [384, 4096], P(('blk', 'grp'))
The draws below stay inside these ranges and needn't reach their ends.
Inputs may be any that keep to these rules, and one draw needn't show every extreme that they name: `flow`: density lies between 1 and 2, pressure between 1 and 2, every velocity component between -1.25 and 1.25. `lateral_owner`: among the faces 0 to 3 of the blocks of one device, at most 9 have their neighbour on any one blk index, and in every draw some device reaches 9.
All inputs are finite; a program needn't handle non-finite values. No bound on the sum of `cut_flag` on one device may be relied on, other than what follows from the above.
Results may differ from the reference program's by a relative error of at most 0.0003.
Values sent between devices are 32-bit elements; how exact they have to be, the bound alone decides.
A program may use at most 128 MiB of HBM per device.

```python
import math
import jax
import jax.numpy as jnp
import numpy as np
from jax import lax

EDGE = 16
BLK_DEV = 12
CELLS = 4096
NB = 384
CAP = 9
N_BLK = 8
N_GRP = 4


def draw_flow(key, part):
    keys = jax.random.split(key, 9)
    grid_shape = (NB, CELLS)
    density = jnp.exp(jax.random.uniform(keys[0], grid_shape, jnp.float32, 0.0, math.log(2.0)))
    pressure = jnp.exp(jax.random.uniform(keys[1], grid_shape, jnp.float32, 0.0, math.log(2.0)))
    velocity = jnp.clip(0.25 * jax.random.normal(keys[2], (3,) + grid_shape, jnp.float32), -0.5, 0.5)
    transonic = jax.random.uniform(keys[3], (NB, 1), jnp.float32) < 0.125
    direction = jax.random.randint(keys[4], (NB, 1), 0, 3)
    heading = jnp.where(jax.random.uniform(keys[5], (NB, 1), jnp.float32) < 0.5, -1.0, 1.0)
    magnitude = jax.random.uniform(keys[6], grid_shape, jnp.float32, 0.75, 1.25)
    fast_density = jax.random.uniform(keys[7], grid_shape, jnp.float32, 1.6, 2.0)
    fast_pressure = jax.random.uniform(keys[8], grid_shape, jnp.float32, 1.0, 1.2)
    density = jnp.where(transonic, fast_density, density)
    pressure = jnp.where(transonic, fast_pressure, pressure)
    component = jnp.arange(3, dtype=jnp.int32)[:, None, None]
    picked = (component == direction[None]) & transonic[None]
    velocity = jnp.where(picked, (heading * magnitude)[None], velocity)
    energy = pressure / 0.4 + 0.5 * density * jnp.sum(velocity * velocity, axis=0)
    return jnp.stack([density, density * velocity[0], density * velocity[1], density * velocity[2], energy], axis=1)


def plant(drawn, rng, low, top_value):
    extent = drawn.shape
    spot = [jax.random.randint(jax.random.fold_in(rng, axis), (), 0, extent[axis]) for axis in range(len(extent))]
    drawn = drawn.at[tuple(spot)].set(low)
    longest = extent.index(max(extent))
    spot[longest] = (spot[longest] + 1) % extent[longest]
    return drawn.at[tuple(spot)].set(top_value)


def level_of(rng, shape, cuts, low, high):
    gain = 1.0
    for axis_at, blocks in cuts:
        steps = jax.random.uniform(jax.random.fold_in(jax.random.fold_in(rng, 6), axis_at), (blocks,), jnp.float32, low / len(cuts), high / len(cuts))
        gain = gain * jnp.repeat(jnp.exp(steps), shape[axis_at] // blocks).reshape((-1,) + (1,) * (len(shape) - 1 - axis_at))
    return gain


def assign_block(key, own, number, rows, number_of, top, reach, slope):
    order = jax.random.permutation(key, number_of)
    heavy_load, common = shares(number_of, rows * top, reach, slope, True), shares(number_of, rows * top, reach, slope, False)
    places = jnp.arange(number_of)

    def named(tallies, offset_by):
        used = int((tallies > 0).sum())
        fixed = max(1, used // 4)
        moved = fixed + (places - fixed + offset_by * (used - fixed)) % max(1, number_of - fixed)
        return jnp.zeros((number_of,), jnp.int32).at[order[jnp.where(places < fixed, places, moved)]].set(jnp.asarray(tallies, jnp.int32))

    tallies = jnp.where(number % 4 == 0, named(heavy_load, number // 4), named(common, number - number // 4 - 1))
    mixed = jax.random.permutation(jax.random.fold_in(own, 3), number_of)
    giver, sink = mixed[0:number_of // 2 * 2:2], mixed[1:number_of // 2 * 2:2]
    slack = jnp.minimum(tallies[giver] - 1, reach - tallies[sink]) // 2
    slack = jnp.where((giver == order[0]) | (sink == order[0]) | (tallies[sink] == 0), 0, jnp.maximum(slack, 0))
    moved = jax.random.randint(jax.random.fold_in(own, 4), (number_of // 2,), 0, 1 << 20) % (slack + 1)
    tallies = tallies.at[giver].add(-moved).at[sink].add(moved)
    labels = jnp.searchsorted(jnp.cumsum(tallies), jnp.arange(rows * top), side="right").astype(jnp.int32)
    table = labels.reshape(top, rows).T
    table = table[jax.random.permutation(jax.random.fold_in(own, 1), rows)]
    offset_by = jax.random.randint(jax.random.fold_in(own, 2), (rows, 1), 0, top)
    return jnp.take_along_axis(table, (jnp.arange(top)[None, :] + offset_by) % top, axis=1)


def shares(count, total, limit, lean, full):
    weights = [(1 << 20) // math.isqrt(standing ** lean) + 1 for standing in range(1, count + 1)]
    largest = limit if full else min(limit, max(-(-total // count), total * weights[0] // sum(weights)))
    least = 1 if total - largest >= count - 1 else 0
    holding, rest = [largest] + [least] * (count - 1), total - largest - least * (count - 1)
    while rest > 0:
        movable = [i for i in range(1, count) if holding[i] < largest] or [i for i in range(1, count) if holding[i] < limit]
        whole, budget = sum([weights[i] for i in movable]), rest
        for i in movable:
            addition = min(limit - holding[i], max(1, budget * weights[i] // whole), rest)
            holding[i] = holding[i] + addition
            rest = rest - addition
    return np.array(holding)


def centred(rng, dims, scale, bound, shards=(), held_as=jnp.bfloat16):
    loudness = level_of(rng, dims, shards, -0.22, 0.18) if shards else 1.0
    values = jax.random.normal(rng, dims, jnp.float32) * scale * loudness
    return jnp.minimum(jnp.maximum(values, -bound), bound).astype(held_as)


def setup_inputs(seed: int = 0) -> dict:
    splits = jax.random.split(jax.random.key(seed), 7)
    flow = draw_flow(jax.random.fold_in(splits[6], 71), 0)
    adjoint = centred(splits[1], (NB, 5, CELLS), 1.0, 6.0, ((0, 32),), jnp.float32)
    cut_flag = plant((jax.random.randint(splits[2], (NB, CELLS), 0, 8) < 1).astype(jnp.int32), jax.random.fold_in(splits[2], 1), 0, 1)
    lateral_owner_keys = jax.random.split(jax.random.fold_in(splits[3], 1), NB * 4 // (4 * BLK_DEV))
    lateral_owner_turns = jax.random.permutation(jax.random.fold_in(splits[3], 3), NB * 4 // (4 * BLK_DEV))
    lateral_owner = jax.vmap(lambda own, number: assign_block(jax.random.fold_in(splits[3], 2), own, number, 4 * BLK_DEV, N_BLK, 1, CAP, 2))(lateral_owner_keys, lateral_owner_turns).reshape((NB, 4, 1))
    lateral_link = plant(jax.random.randint(splits[4], (NB, 4), 0, 5 * BLK_DEV), jax.random.fold_in(splits[4], 1), 0, (5 * BLK_DEV) - 1).astype(jnp.int32)
    vertical_link = plant(jax.random.randint(splits[5], (NB, 2), 0, 5 * BLK_DEV), jax.random.fold_in(splits[5], 1), 0, (5 * BLK_DEV) - 1).astype(jnp.int32)
    return {"flow": flow, "adjoint": adjoint, "cut_flag": cut_flag, "lateral_owner": lateral_owner, "lateral_link": lateral_link, "vertical_link": vertical_link}


HEAT_RATIO = 1.4
ENTROPY_FIX = 0.2
FREESTREAM = (1.0, 0.0, 0.0, 0.3, 1.0)

def primitive(conserved):
    density = conserved[:, 0]
    velocity = conserved[:, 1:4] / density[:, None]
    pressure = (HEAT_RATIO - 1.0) * (conserved[:, 4] - 0.5 * density * lax.optimization_barrier(jnp.sum(velocity * velocity, axis=1)))
    return jnp.concatenate([density[:, None], velocity, pressure[:, None]], axis=1)

def minmod(first_diff, second_diff):
    return jnp.where(first_diff * second_diff > 0.0, jnp.sign(first_diff) * jnp.minimum(jnp.abs(first_diff), jnp.abs(second_diff)), 0.0)

def harten(wave_rate, spread):
    return jnp.where(wave_rate < spread, (wave_rate * wave_rate + spread * spread) / (2.0 * spread), wave_rate)

def roe_flux(left_state, right_state, normal_axis):
    left_rho = left_state[0]
    right_rho = right_state[0]
    left_vel = left_state[1:4]
    right_vel = right_state[1:4]
    left_press = left_state[4]
    right_press = right_state[4]
    factor = HEAT_RATIO / (HEAT_RATIO - 1.0)
    left_enth = factor * left_press / left_rho + 0.5 * lax.optimization_barrier(jnp.sum(left_vel * left_vel, axis=0))
    right_enth = factor * right_press / right_rho + 0.5 * lax.optimization_barrier(jnp.sum(right_vel * right_vel, axis=0))
    left_root = jnp.sqrt(left_rho)
    right_root = jnp.sqrt(right_rho)
    weight_sum = left_root + right_root
    mean_vel = (left_root * left_vel + right_root * right_vel) / weight_sum
    mean_enth = (left_root * left_enth + right_root * right_enth) / weight_sum
    speed_sq = lax.optimization_barrier(jnp.sum(mean_vel * mean_vel, axis=0))
    sound_sq = (HEAT_RATIO - 1.0) * (mean_enth - 0.5 * speed_sq)
    sound_speed = jnp.sqrt(sound_sq)
    mean_rho = left_root * right_root
    normal = mean_vel[normal_axis]
    jump_vel = right_vel - left_vel
    jump_rho = right_rho - left_rho
    jump_press = right_press - left_press
    jump_normal = jump_vel[normal_axis]
    wave_slow = (jump_press - mean_rho * sound_speed * jump_normal) / (2.0 * sound_sq)
    wave_fast = (jump_press + mean_rho * sound_speed * jump_normal) / (2.0 * sound_sq)
    wave_entropy = jump_rho - jump_press / sound_sq
    spread = ENTROPY_FIX * sound_speed
    slow_part = harten(jnp.abs(normal - sound_speed), spread) * wave_slow
    fast_part = harten(jnp.abs(normal + sound_speed), spread) * wave_fast
    mid_part = jnp.abs(normal) * wave_entropy
    shear_part = jnp.abs(normal) * mean_rho
    unit_vector = [1.0 if axis_no == normal_axis else 0.0 for axis_no in range(3)]
    shear_jump = [jump_vel[axis_no] - jump_normal * unit_vector[axis_no] for axis_no in range(3)]
    diss_mass = slow_part + fast_part + mid_part
    diss_mom = [slow_part * (mean_vel[axis_no] - sound_speed * unit_vector[axis_no]) + fast_part * (mean_vel[axis_no] + sound_speed * unit_vector[axis_no]) + mid_part * mean_vel[axis_no] + shear_part * shear_jump[axis_no] for axis_no in range(3)]
    diss_energy = slow_part * (mean_enth - normal * sound_speed) + fast_part * (mean_enth + normal * sound_speed) + mid_part * 0.5 * speed_sq + shear_part * (mean_vel[0] * shear_jump[0] + mean_vel[1] * shear_jump[1] + mean_vel[2] * shear_jump[2])
    left_normal = left_vel[normal_axis]
    right_normal = right_vel[normal_axis]
    mass_flux = 0.5 * (left_rho * left_normal + right_rho * right_normal) - 0.5 * diss_mass
    momentum = [0.5 * (left_rho * left_normal * left_vel[axis_no] + right_rho * right_normal * right_vel[axis_no] + (left_press + right_press) * unit_vector[axis_no]) - 0.5 * diss_mom[axis_no] for axis_no in range(3)]
    energy = 0.5 * (left_rho * left_normal * left_enth + right_rho * right_normal * right_enth) - 0.5 * diss_energy
    return jnp.stack([mass_flux] + momentum + [energy], axis=0)

def wall_flux(pressure, normal_axis):
    nothing = jnp.zeros_like(pressure)
    parts = [pressure if axis_no == normal_axis else nothing for axis_no in range(3)]
    return jnp.stack([nothing] + parts + [nothing], axis=0)

def face_flux(left_state, right_state, left_solid, right_solid, normal_axis):
    roe_value = roe_flux(left_state, right_state, normal_axis)
    from_left = (right_solid > 0.5) & (left_solid < 0.5)
    from_right = (left_solid > 0.5) & (right_solid < 0.5)
    return jnp.where(from_left, wall_flux(left_state[4], normal_axis), jnp.where(from_right, wall_flux(right_state[4], normal_axis), roe_value))

def faces_of(coarse_cube):
    face_shape = (coarse_cube.shape[0], coarse_cube.shape[1], EDGE * EDGE)
    return jnp.stack([coarse_cube[:, :, 0].reshape(face_shape), coarse_cube[:, :, -1].reshape(face_shape), coarse_cube[:, :, :, 0].reshape(face_shape), coarse_cube[:, :, :, -1].reshape(face_shape), coarse_cube[:, :, :, :, 0].reshape(face_shape), coarse_cube[:, :, :, :, -1].reshape(face_shape)], axis=1)

def select_face(face_slab, level_code):
    channels = face_slab.shape[0]
    half_edge = EDGE // 2
    square = face_slab.reshape(channels, EDGE, EDGE)
    quarter_code = jnp.minimum(level_code, 3)
    anchor = jnp.zeros((), jnp.int32)
    first_start = (quarter_code // 2 * half_edge).astype(jnp.int32)
    second_start = (quarter_code % 2 * half_edge).astype(jnp.int32)
    quarter = lax.dynamic_slice(square, (anchor, first_start, second_start), (channels, half_edge, half_edge))
    widened = jnp.broadcast_to(quarter[:, :, None, :, None], (channels, half_edge, 2, half_edge, 2))
    return jnp.where(level_code == 4, face_slab, widened.reshape(channels, EDGE * EDGE))

def prolong(coarse_cube, ghosts):
    channels = coarse_cube.shape[0]
    edge_cells = coarse_cube.shape[1]
    slopes = []
    for axis_no in range(3):
        dim_no = axis_no + 1
        lower_side = jnp.concatenate([jnp.expand_dims(ghosts[2 * axis_no], dim_no), lax.slice_in_dim(coarse_cube, 0, edge_cells - 1, axis=dim_no)], axis=dim_no)
        upper_side = jnp.concatenate([lax.slice_in_dim(coarse_cube, 1, edge_cells, axis=dim_no), jnp.expand_dims(ghosts[2 * axis_no + 1], dim_no)], axis=dim_no)
        slopes.append(minmod(upper_side - coarse_cube, coarse_cube - lower_side))
    split_shape = (channels, edge_cells, 1, edge_cells, 1, edge_cells, 1)
    child_signs = jnp.array([-0.25, 0.25], jnp.float32)
    fine_field = coarse_cube.reshape(split_shape) + slopes[0].reshape(split_shape) * child_signs[:, None, None, None, None] + slopes[1].reshape(split_shape) * child_signs[:, None, None] + slopes[2].reshape(split_shape) * child_signs
    return fine_field.reshape(channels, 2 * edge_cells, 2 * edge_cells, 2 * edge_cells)

def residual(fine_field, fine_ghosts, solid_mask):
    size_fine = fine_field.shape[1]
    summed = jnp.zeros_like(fine_field)
    for axis_no in range(3):
        dim_no = axis_no + 1
        left_state = jnp.concatenate([jnp.expand_dims(fine_ghosts[2 * axis_no], dim_no), fine_field], axis=dim_no)
        right_state = jnp.concatenate([fine_field, jnp.expand_dims(fine_ghosts[2 * axis_no + 1], dim_no)], axis=dim_no)
        open_rim = jnp.expand_dims(jnp.zeros((size_fine, size_fine), jnp.float32), axis_no)
        left_solid = jnp.concatenate([open_rim, solid_mask], axis=axis_no)
        right_solid = jnp.concatenate([solid_mask, open_rim], axis=axis_no)
        flux_all = face_flux(left_state, right_state, left_solid, right_solid, axis_no)
        summed = summed + lax.slice_in_dim(flux_all, 1, size_fine + 1, axis=dim_no) - lax.slice_in_dim(flux_all, 0, size_fine, axis=dim_no)
    return jnp.where(solid_mask[None] > 0.5, 0.0, summed)

def block_indicator(operands):
    flow_prim, adjoint_block, ghosts, flags = operands
    coarse_flow = flow_prim.reshape(5, EDGE, EDGE, EDGE)
    coarse_adjoint = adjoint_block.reshape(5, EDGE, EDGE, EDGE)
    face_ghosts = ghosts.reshape(6, 10, EDGE, EDGE)
    fine_flow = prolong(coarse_flow, face_ghosts[:, :5])
    fine_adjoint = prolong(coarse_adjoint, face_ghosts[:, 5:])
    wide_ghosts = jnp.broadcast_to(face_ghosts[:, :5, :, None, :, None], (6, 5, EDGE, 2, EDGE, 2)).reshape(6, 5, 2 * EDGE, 2 * EDGE)
    solid_mask = jnp.broadcast_to(flags.astype(jnp.float32).reshape(EDGE, 1, EDGE, 1, EDGE, 1), (EDGE, 2, EDGE, 2, EDGE, 2)).reshape(2 * EDGE, 2 * EDGE, 2 * EDGE)
    fine_residual = residual(fine_flow, wide_ghosts, solid_mask)
    weighted = lax.optimization_barrier(jnp.sum(fine_adjoint * fine_residual, axis=0))
    coarse = weighted.reshape(EDGE, 2, EDGE, 2, EDGE, 2).sum(axis=(1, 3, 5))
    return jnp.abs(coarse).reshape(EDGE * EDGE * EDGE)

def reference(flow, adjoint, cut_flag, lateral_owner, lateral_link, vertical_link):
    number_blocks = flow.shape[0]
    primitives = primitive(flow)
    coarse_both = jnp.concatenate([primitives, adjoint], axis=1).reshape(number_blocks, 10, EDGE, EDGE, EDGE)
    face_all = faces_of(coarse_both)
    block_ids = jnp.arange(number_blocks, dtype=jnp.int32)
    device_ids = block_ids // BLK_DEV
    region = device_ids % N_GRP
    column = device_ids // N_GRP
    lateral_block = (lateral_owner[:, :, 0] * N_GRP + region[:, None]) * BLK_DEV + lateral_link // 5
    opposite = jnp.array([1, 0, 3, 2], jnp.int32)
    lateral_slab = face_all[lateral_block, opposite[None, :]]
    lateral_ghost = jax.vmap(jax.vmap(select_face))(lateral_slab, lateral_link % 5)
    lower_region = jnp.maximum(region - 1, 0)
    upper_region = jnp.minimum(region + 1, N_GRP - 1)
    lower_block = (column * N_GRP + lower_region) * BLK_DEV + vertical_link[:, 0] // 5
    upper_block = (column * N_GRP + upper_region) * BLK_DEV + vertical_link[:, 1] // 5
    lower_ghost = jax.vmap(select_face)(face_all[lower_block, 5], vertical_link[:, 0] % 5)
    upper_ghost = jax.vmap(select_face)(face_all[upper_block, 4], vertical_link[:, 1] % 5)
    state = jnp.array(FREESTREAM, jnp.float32)
    farfield_layer = jnp.concatenate([jnp.broadcast_to(state[:, None], (5, EDGE * EDGE)), jnp.zeros((5, EDGE * EDGE), jnp.float32)], axis=0)
    lower_ghost = jnp.where((region == 0)[:, None, None], farfield_layer, lower_ghost)
    upper_ghost = jnp.where((region == N_GRP - 1)[:, None, None], farfield_layer, upper_ghost)
    ghosts = jnp.concatenate([lateral_ghost, lower_ghost[:, None], upper_ghost[:, None]], axis=1)
    return lax.map(block_indicator, (primitives, adjoint, ghosts, cut_flag))
```

```python
import functools

import jax
import jax.numpy as jnp
from jax import lax
from jax.experimental import pallas as pl
from jax.experimental.pallas import tpu as pltpu
from jax.sharding import PartitionSpec as P

EDGE = 16
PLANE = EDGE * EDGE
LANES = 128
PACK = 4
FREESTREAM = (1.0, 0.0, 0.0, 0.3, 1.0)
VMEM = pl.BlockSpec(memory_space=pltpu.VMEM)
SMEM = pl.BlockSpec(memory_space=pltpu.SMEM)


def iota(shape, dim):
    return lax.broadcasted_iota(jnp.int32, shape, dim)


def primitive(state):
    density, mom, energy = state[0], state[1:4], state[4]
    root = lax.rsqrt(density)
    inverse = root * root
    vel = [m * inverse for m in mom]
    square = vel[0] * vel[0] + vel[1] * vel[1] + vel[2] * vel[2]
    return [density, *vel, 0.4 * (energy - 0.5 * density * square)]


def faces_kernel(flow_ref, adj_ref, lat_ref, ver_ref):
    blocks = flow_ref.shape[1]
    lane = iota((blocks, LANES), 1)
    slot, spot = lane >> 4, lane & 15

    def layers(ref, c):
        def tile(i, half):
            return ref[c, :, i * PLANE + half * LANES : i * PLANE + (half + 1) * LANES]

        out = {}
        for half in range(2):
            out[0, half] = tile(0, half)
            out[1, half] = tile(EDGE - 1, half)
            low_j = high_j = low_k = high_k = jnp.zeros((blocks, LANES), jnp.float32)
            for i in range(EDGE):
                if i // 8 == half:
                    il = i % 8
                    low_j = jnp.where(slot == il, pltpu.roll(tile(i, 0), il * 16, 1), low_j)
                    high_j = jnp.where(
                        slot == il, pltpu.roll(tile(i, 1), (il * 16 + 16) % LANES, 1), high_j
                    )
                here = tile(i, half)
                low_k = jnp.where(spot == i, pltpu.roll(here, i, 1), low_k)
                high_k = jnp.where(spot == i, pltpu.roll(here, (LANES + i - 15) % LANES, 1), high_k)
            out[2, half], out[3, half], out[4, half], out[5, half] = low_j, high_j, low_k, high_k
        return out

    def put(face, half, c, value):
        where = slice(half * LANES, (half + 1) * LANES)
        if face < 4:
            lat_ref[face, c, :, where] = value
        else:
            ver_ref[face - 4, c, :, where] = value

    for c in range(5):
        for (face, half), value in layers(flow_ref, c).items():
            put(face, half, c, value)
        for (face, half), value in layers(adj_ref, c).items():
            put(face, half, 5 + c, value)
    for half in range(2):
        where = slice(half * LANES, (half + 1) * LANES)
        for ref, count in ((lat_ref, 4), (ver_ref, 2)):
            for face in range(count):
                prim = primitive([ref[face, c, :, where] for c in range(5)])
                for c in range(1, 5):
                    ref[face, c, :, where] = prim[c]


def gather_kernel(index_ref, lat_ref, out_ref):
    def one(r, carry):
        code = index_ref[r]
        face, block = code & 3, code >> 2
        for c in range(10):
            out_ref[pl.ds(r * 10 + c, 1), :] = lat_ref[face, c, pl.ds(block, 1), :]
        return carry

    lax.fori_loop(0, index_ref.shape[0], one, 0)


def minmod(a, b):
    return jnp.where(a * b > 0.0, jnp.where(jnp.abs(a) < jnp.abs(b), a, b), 0.0)


def derive(state):
    rho, u, v, w, p = state
    inv_root = lax.rsqrt(rho)
    root = rho * inv_root
    enth = (3.5 * p) * (inv_root * inv_root) + 0.5 * (u * u + v * v + w * w)
    return (rho, (u, v, w), p, enth, root, (root * u, root * v, root * w), root * enth)


def roe(left, right, n):
    rho_l, vel_l, p_l, h_l, root_l, rv_l, rh_l = left
    rho_r, vel_r, p_r, h_r, root_r, rv_r, rh_r = right
    t1, t2 = [a for a in range(3) if a != n]
    r = lax.rsqrt(root_l + root_r)
    inv = r * r
    vel = [(a + b) * inv for a, b in zip(rv_l, rv_r)]
    enth = (rh_l + rh_r) * inv
    half_sq = 0.5 * (vel[0] * vel[0] + vel[1] * vel[1] + vel[2] * vel[2])
    c_sq = 0.4 * (enth - half_sq)
    inv_c = lax.rsqrt(c_sq)
    c = c_sq * inv_c
    inv_c_sq = inv_c * inv_c
    rho = root_l * root_r
    un = vel[n]
    dp = p_r - p_l
    scaled = dp * inv_c_sq
    half = 0.5 * scaled
    jump = (0.5 * (rho * inv_c)) * (vel_r[n] - vel_l[n])
    spread, tenth, factor = 0.2 * c, 0.1 * c, 2.5 * inv_c

    def rate(x):
        x = jnp.abs(x)
        return jnp.where(x < spread, x * x * factor + tenth, x)

    slow = rate(un - c) * (half - jump)
    fast = rate(un + c) * (half + jump)
    speed = jnp.abs(un)
    mid = speed * ((rho_r - rho_l) - scaled)
    shear = speed * rho
    both = slow + fast
    diff = c * (fast - slow)
    mass = both + mid
    s1 = shear * (vel_r[t1] - vel_l[t1])
    s2 = shear * (vel_r[t2] - vel_l[t2])
    m_l, m_r = rho_l * vel_l[n], rho_r * vel_r[n]
    out = [None] * 5
    out[0] = m_l + m_r - mass
    out[1 + n] = m_l * vel_l[n] + m_r * vel_r[n] + (p_l + p_r) - (un * mass + diff)
    out[1 + t1] = m_l * vel_l[t1] + m_r * vel_r[t1] - (vel[t1] * mass + s1)
    out[1 + t2] = m_l * vel_l[t2] + m_r * vel_r[t2] - (vel[t2] * mass + s2)
    out[4] = (
        m_l * h_l + m_r * h_r
        - (enth * both + un * diff + mid * half_sq + vel[t1] * s1 + vel[t2] * s2)
    )
    return out


def quads(base, q1, q2):
    low = [b - q for b, q in zip(base, q1)]
    high = [b + q for b, q in zip(base, q1)]
    return [
        derive([b - q for b, q in zip(low, q2)]),
        derive([b + q for b, q in zip(low, q2)]),
        derive([b - q for b, q in zip(high, q2)]),
        derive([b + q for b, q in zip(high, q2)]),
    ]


def moments(lefts, rights, n):
    f = [roe(a, b, n) for a, b in zip(lefts, rights)]
    zero, first, second = [], [], []
    for c in range(5):
        low, high = f[0][c] + f[1][c], f[2][c] + f[3][c]
        zero.append(low + high)
        first.append(high - low)
        second.append((f[1][c] - f[0][c]) + (f[3][c] - f[2][c]))
    return zero + first + second


def dot(a, b):
    total = a[0] * b[0]
    for x, y in zip(a[1:], b[1:]):
        total = total + x * y
    return total


def main_kernel(
    row_ref, slot_ref, edge_ref,
    flow_ref, adj_ref, flag_ref, code_ref, ret_ref, low_ref, high_ref,
    out_ref,
    val, slope, solid, ghost, low_k, low_j, mom_k, mom_j, mom_i, lo_solid,
):
    blocks = flow_ref.shape[1]
    groups = blocks // PACK
    lane = iota((8, LANES), 1)
    row = iota((8, LANES), 0)
    top = row < PACK
    slot, spot = lane >> 4, lane & 15

    def pack(parts):
        tiles = []
        for g in range(groups):
            at = g * PACK % 8
            first, second = parts[g * PACK // 8]
            if first.shape[0] == PACK:
                tiles.append(jnp.concatenate([first, second], axis=0))
            elif at == 0:
                tiles.append(jnp.where(top, first, pltpu.roll(second, 4, 0)))
            else:
                tiles.append(jnp.where(top, pltpu.roll(first, 4, 0), second))
        return tiles

    def read(load, i):
        parts = []
        for start in range(0, blocks, 8):
            rows = slice(start, min(start + 8, blocks))
            parts.append(
                [load(rows, pl.ds(pl.multiple_of(i * PLANE + h * LANES, LANES), LANES)) for h in range(2)]
            )
        return pack(parts)

    def load_layer(i, carry):
        flow = [read(lambda r, s: flow_ref[c, r, s], i) for c in range(5)]
        for g in range(groups):
            for c, x in enumerate(primitive([f[g] for f in flow])):
                val[g, c, 1 + i] = x
        for c in range(5):
            for g, x in enumerate(read(lambda r, s: adj_ref[c, r, s], i)):
                val[g, 5 + c, 1 + i] = x
        for g, x in enumerate(read(lambda r, s: flag_ref[r, s], i)):
            solid[g, 1 + i] = x.astype(jnp.float32)
        return carry

    lax.fori_loop(0, EDGE, load_layer, 0)

    def load_ghost(c, carry):
        for b in range(blocks):
            g, at = b // PACK, b % PACK
            for f in range(6):
                if f < 4:
                    x = ret_ref[pl.ds(row_ref[b * 4 + f] * 10 + c, 1), :]
                else:
                    ref = low_ref if f == 4 else high_ref
                    x = ref[c, pl.ds(slot_ref[b * 2 + f - 4], 1), :]
                ghost[g, f, c, at : at + 1, :] = x[:, :LANES]
                ghost[g, f, c, PACK + at : PACK + at + 1, :] = x[:, LANES:]
        return carry

    lax.fori_loop(0, 10, load_ghost, 0)
    upper_half = 1 - (row >> 2)
    for g in range(groups):
        for f in range(6):
            code = code_ref[f, g]
            half = 1 - upper_half
            own = (code == 4) | ((code >> 1) == half)
            quarter = ((4 * half + (slot >> 1)) << 4) + ((code & 1) << 3) + (spot >> 1)
            index = jnp.where(code == 4, lane, quarter)
            for c in range(10):
                x = ghost[g, f, c]
                x = jnp.where(own, x, pltpu.roll(x, 4, 0))
                x = jnp.take_along_axis(x, index, axis=1, mode="promise_in_bounds")
                if f >= 4:
                    far = FREESTREAM[c] if c < 5 else 0.0
                    x = jnp.where(edge_ref[f - 4] == 1, far, x)
                ghost[g, f, c] = x
    for g in range(groups):
        nothing = jnp.zeros((8, LANES), jnp.float32)
        solid[g, 0] = nothing
        solid[g, EDGE + 1] = nothing
        for c in range(10):
            val[g, c, 0] = ghost[g, 0, c]
            val[g, c, EDGE + 1] = ghost[g, 1, c]
    for d in range(3):
        for c in range(5):
            nothing = jnp.zeros((8, LANES), jnp.float32)
            slope[d, c, 0] = nothing
            slope[d, c, EDGE + 1] = nothing

    def next_k(x, edge, i):
        edge = 0.0 if edge is None else pltpu.roll(edge, 15 - i, 1)
        return jnp.where(spot == 15, edge, pltpu.roll(x, LANES - 1, 1))

    def prev_k(x, edge, i):
        edge = 0.0 if edge is None else pltpu.roll(edge, (LANES - i) % LANES, 1)
        return jnp.where(spot == 0, edge, pltpu.roll(x, 1, 1))

    def place(edge, i, lane_at, upper):
        if edge is None:
            return 0.0
        edge = pltpu.roll(edge, (2 * LANES + lane_at - (i & 7) * 16) % LANES, 1)
        same = (i >> 3) == (1 if upper else 0)
        return jnp.where(same, edge, pltpu.roll(edge, 4, 0))

    def next_j(x, edge, i):
        y = pltpu.roll(x, LANES - 16, 1)
        z = jnp.where(top, pltpu.roll(y, 4, 0), place(edge, i, LANES - 16, True))
        return jnp.where(slot == 7, z, y)

    def prev_j(x, edge, i):
        y = pltpu.roll(x, 16, 1)
        z = jnp.where(top, place(edge, i, 0, False), pltpu.roll(y, 4, 0))
        return jnp.where(slot == 0, z, y)

    def group(g, carry):
        def slopes(i, inner):
            at_k = spot == i
            at_j = ((row >> 2) == (i >> 3)) & (slot == (i & 7))
            for c in range(10):
                own = val[g, c, 1 + i]
                found = [
                    minmod(val[g, c, 2 + i] - own, own - val[g, c, i]),
                    minmod(next_j(own, ghost[g, 3, c], i) - own, own - prev_j(own, ghost[g, 2, c], i)),
                    minmod(next_k(own, ghost[g, 5, c], i) - own, own - prev_k(own, ghost[g, 4, c], i)),
                ]
                found = [0.25 * s for s in found]
                for d in range(3):
                    slope[d, c, 1 + i] = found[d]
                if c < 5:
                    for d, x in enumerate([own, *found]):
                        low_k[d, c] = jnp.where(at_k, pltpu.roll(x, i, 1), low_k[d, c])
                        x = jnp.where(top, x, pltpu.roll(x, 4, 0))
                        low_j[d, c] = jnp.where(at_j, pltpu.roll(x, (i & 7) * 16, 1), low_j[d, c])
            return inner

        lax.fori_loop(0, EDGE, slopes, 0)

        def first_faces(n, lower, cell):
            t1, t2 = [a for a in range(3) if a != n]
            left = derive(lower)
            base = [cell(0, c) - cell(1 + n, c) for c in range(5)]
            rights = quads(base, [cell(1 + t1, c) for c in range(5)], [cell(1 + t2, c) for c in range(5)])
            return moments([left] * 4, rights, n)

        for ref, n in ((mom_j, 1), (mom_k, 2)):
            source = low_j if n == 1 else low_k
            found = first_faces(n, [ghost[g, 2 * n, c] for c in range(5)], lambda d, c: source[d, c])
            for c in range(15):
                ref[c] = found[c]
        found = first_faces(
            0,
            [ghost[g, 0, c] for c in range(5)],
            lambda d, c: val[g, c, 1] if d == 0 else slope[d - 1, c, 1],
        )
        for c in range(15):
            mom_i[c] = found[c]

        def layer(i, inner):
            v = [val[g, c, 1 + i] for c in range(5)]
            q = [[slope[d, c, 1 + i] for c in range(5)] for d in range(3)]
            av = [val[g, 5 + c, 1 + i] for c in range(5)]
            aq = [[slope[d, 5 + c, 1 + i] for c in range(5)] for d in range(3)]
            child = {}
            for a in range(2):
                base = [x + y if a else x - y for x, y in zip(v, q[0])]
                for at, state in enumerate(quads(base, q[1], q[2])):
                    child[a, at >> 1, at & 1] = state

            def side(n, high):
                order = [(s, t) for s in range(2) for t in range(2)]
                return [child[tuple([*st[:n], high, *st[n:]])] for st in order]

            own_solid = solid[g, 1 + i]
            total = jnp.zeros((8, LANES), jnp.float32)
            for n in range(3):
                t1, t2 = [a for a in range(3) if a != n]
                f = [roe(a, b, n) for a, b in zip(side(n, 0), side(n, 1))]
                inside = [(f[0][c] + f[1][c]) + (f[2][c] + f[3][c]) for c in range(5)]
                total = total - 2.0 * dot(aq[n], inside)
                if n == 0:
                    base = [val[g, c, 2 + i] - slope[0, c, 2 + i] for c in range(5)]
                    q1 = [slope[1, c, 2 + i] for c in range(5)]
                    q2 = [slope[2, c, 2 + i] for c in range(5)]
                    up_solid, down_solid = solid[g, 2 + i], solid[g, i]
                else:
                    ahead, behind = (next_j, prev_j) if n == 1 else (next_k, prev_k)
                    base = [ahead(v[c] - q[n][c], ghost[g, 2 * n + 1, c], i) for c in range(5)]
                    q1 = [ahead(q[t1][c], None, i) for c in range(5)]
                    q2 = [ahead(q[t2][c], None, i) for c in range(5)]
                    up_solid, down_solid = ahead(own_solid, None, i), behind(own_solid, None, i)
                above = moments(side(n, 1), quads(base, q1, q2), n)
                if n == 0:
                    below = [mom_i[c] for c in range(15)]
                    for c in range(15):
                        mom_i[c] = above[c]
                else:
                    first = mom_j if n == 1 else mom_k
                    below = [behind(above[c], first[c], i) for c in range(15)]
                outer = [x + y for x, y in zip(av, aq[n])]
                inner_side = [x - y for x, y in zip(av, aq[n])]
                upper = dot([*outer, *aq[t1], *aq[t2]], above)
                lower = dot([*inner_side, *aq[t1], *aq[t2]], below)
                cross = aq[t1][1 + n] * q[t1][4] + aq[t2][1 + n] * q[t2][4]
                wall_up = 8.0 * (outer[1 + n] * (v[4] + q[n][4]) + cross)
                wall_down = 8.0 * (inner_side[1 + n] * (v[4] - q[n][4]) + cross)
                total = total + (
                    jnp.where(up_solid > 0.5, wall_up, upper)
                    - jnp.where(down_solid > 0.5, wall_down, lower)
                )
            total = jnp.where(own_solid > 0.5, 0.0, 0.5 * jnp.abs(total))
            lo_solid[g, i] = total
            return inner

        lax.fori_loop(0, EDGE, layer, 0)
        return carry

    lax.fori_loop(0, groups, group, 0)

    def store(i, carry):
        for g in range(groups):
            x = lo_solid[g, i]
            for h in range(2):
                out_ref[
                    g * PACK : (g + 1) * PACK,
                    pl.ds(pl.multiple_of(i * PLANE + h * LANES, LANES), LANES),
                ] = x[h * PACK : (h + 1) * PACK]
        return carry

    lax.fori_loop(0, EDGE, store, 0)


def local(flow, adjoint, cut_flag, lateral_owner, lateral_link, vertical_link):
    blocks = flow.shape[0]
    groups = blocks // PACK
    peers = lax.axis_size("blk")
    capacity = max(2, 6 * blocks // peers)
    flow_t = jnp.transpose(flow, (1, 0, 2))
    adj_t = jnp.transpose(adjoint, (1, 0, 2))
    f32 = functools.partial(jax.ShapeDtypeStruct, dtype=jnp.float32)

    owners = lateral_owner[:, :, 0].reshape(-1)
    links = lateral_link.reshape(-1)
    count = blocks * 4
    order = jnp.arange(count, dtype=jnp.int32)
    wanted_face = links // 5 * 4 + ((order % 4) ^ 1)
    earlier = (owners[None, :] == owners[:, None]) & (order[None, :] < order[:, None])
    position = jnp.sum(earlier.astype(jnp.int32), axis=1)
    place = owners * capacity + position
    hit = place[None, :] == jnp.arange(peers * capacity, dtype=jnp.int32)[:, None]
    requests = jnp.sum(jnp.where(hit, wanted_face[None, :], 0), axis=1).reshape(peers, capacity)
    wanted = lax.all_to_all(requests, "blk", split_axis=0, concat_axis=0, tiled=True).reshape(-1)

    lateral, vertical = pl.pallas_call(
        faces_kernel,
        out_shape=(f32((4, 10, blocks, PLANE)), f32((2, 10, blocks, PLANE))),
        in_specs=[VMEM, VMEM],
        out_specs=(VMEM, VMEM),
        name="faces",
    )(flow_t, adj_t)

    regions = lax.axis_size("grp")
    region = lax.axis_index("grp")
    from_low = lax.ppermute(vertical[1], "grp", [(r, r + 1) for r in range(regions - 1)])
    from_high = lax.ppermute(vertical[0], "grp", [(r + 1, r) for r in range(regions - 1)])

    replies = pl.pallas_call(
        gather_kernel,
        out_shape=f32((peers * capacity * 10, PLANE)),
        in_specs=[SMEM, VMEM],
        out_specs=VMEM,
        name="gather",
    )(wanted, lateral)
    returned = lax.all_to_all(
        replies.reshape(peers, capacity * 10, PLANE), "blk", split_axis=0, concat_axis=0, tiled=True
    ).reshape(peers * capacity * 10, PLANE)

    ver_code = vertical_link % 5
    ver_code = jnp.where(ver_code == 4, 4, ver_code % 2 * 2 + ver_code // 2)
    codes = jnp.concatenate([lateral_link % 5, ver_code], axis=1)
    codes = codes.reshape(groups, 1, PACK, 6).transpose(3, 0, 1, 2)
    codes = jnp.broadcast_to(codes, (6, groups, 2, PACK)).reshape(6, groups, 8, 1)
    codes = jnp.broadcast_to(codes, (6, groups, 8, LANES))
    edges = jnp.stack([region == 0, region == regions - 1]).astype(jnp.int32)

    tile = functools.partial(pltpu.VMEM, dtype=jnp.float32)
    return pl.pallas_call(
        main_kernel,
        out_shape=f32((blocks, EDGE * PLANE)),
        in_specs=[SMEM] * 3 + [VMEM] * 7,
        out_specs=VMEM,
        scratch_shapes=[
            tile((groups, 10, EDGE + 2, 8, LANES)),
            tile((3, 10, EDGE + 2, 8, LANES)),
            tile((groups, EDGE + 2, 8, LANES)),
            tile((groups, 6, 10, 8, LANES)),
            tile((4, 5, 8, LANES)),
            tile((4, 5, 8, LANES)),
            tile((15, 8, LANES)),
            tile((15, 8, LANES)),
            tile((15, 8, LANES)),
            tile((groups, EDGE, 8, LANES)),
        ],
        compiler_params=pltpu.CompilerParams(vmem_limit_bytes=50 * 1024 * 1024),
        name="indicator",
    )(
        place, (vertical_link // 5).reshape(-1), edges,
        flow_t, adj_t, cut_flag, codes, returned, from_low, from_high,
    )


def solution(mesh):
    spec3 = P(("blk", "grp"), None, None)
    spec2 = P(("blk", "grp"), None)
    return jax.shard_map(
        local,
        mesh=mesh,
        in_specs=(spec3, spec3, spec2, spec3, spec2, spec2),
        out_specs=spec2,
        check_vma=False,
    )
```

```python
import functools

import jax
import jax.numpy as jnp
from jax import lax
from jax.experimental import pallas as pl
from jax.experimental.pallas import tpu as pltpu
from jax.sharding import PartitionSpec as P

EDGE = 16
PLANE = EDGE * EDGE
LANES = 128
PACK = 4
FREESTREAM = (1.0, 0.0, 0.0, 0.3, 1.0)
VMEM = pl.BlockSpec(memory_space=pltpu.VMEM)
SMEM = pl.BlockSpec(memory_space=pltpu.SMEM)
MESH = pl.DeviceIdType.MESH


def iota(shape, dim):
    return lax.broadcasted_iota(jnp.int32, shape, dim)


def primitive(state):
    density, mom, energy = state[0], state[1:4], state[4]
    root = lax.rsqrt(density)
    inverse = root * root
    vel = [m * inverse for m in mom]
    square = vel[0] * vel[0] + vel[1] * vel[1] + vel[2] * vel[2]
    return [density, *vel, 0.4 * (energy - 0.5 * density * square)]


def faces_kernel(req_ref, flow_ref, adj_ref, lat_ref, ver_ref, want_ref, send_sem, recv_sem, own_sem):
    blocks = flow_ref.shape[1]
    peers = req_ref.shape[0]
    me = lax.axis_index("blk")

    def copy(d):
        peer = lax.rem(me + d, peers)
        return pltpu.make_async_remote_copy(
            src_ref=req_ref.at[peer],
            dst_ref=want_ref.at[me],
            send_sem=send_sem.at[d],
            recv_sem=recv_sem.at[d],
            device_id={"blk": peer},
            device_id_type=MESH,
        )

    barrier = pltpu.get_barrier_semaphore()
    for d in range(1, peers):
        pl.semaphore_signal(
            barrier, inc=1, device_id={"blk": lax.rem(me + d, peers)}, device_id_type=MESH
        )
    own = pltpu.make_async_copy(req_ref.at[me], want_ref.at[me], own_sem)
    own.start()
    lane = iota((blocks, LANES), 1)
    slot, spot = lane >> 4, lane & 15

    def layers(ref, c):
        def tile(i, half):
            return ref[c, :, i * PLANE + half * LANES : i * PLANE + (half + 1) * LANES]

        out = {}
        for half in range(2):
            out[0, half] = tile(0, half)
            out[1, half] = tile(EDGE - 1, half)
            low_j = high_j = low_k = high_k = jnp.zeros((blocks, LANES), jnp.float32)
            for i in range(EDGE):
                if i // 8 == half:
                    il = i % 8
                    low_j = jnp.where(slot == il, pltpu.roll(tile(i, 0), il * 16, 1), low_j)
                    high_j = jnp.where(
                        slot == il, pltpu.roll(tile(i, 1), (il * 16 + 16) % LANES, 1), high_j
                    )
                here = tile(i, half)
                low_k = jnp.where(spot == i, pltpu.roll(here, i, 1), low_k)
                high_k = jnp.where(spot == i, pltpu.roll(here, (LANES + i - 15) % LANES, 1), high_k)
            out[2, half], out[3, half], out[4, half], out[5, half] = low_j, high_j, low_k, high_k
        return out

    def put(face, half, c, value):
        where = slice(half * LANES, (half + 1) * LANES)
        if face < 4:
            lat_ref[face, c, :, where] = value
        else:
            ver_ref[face - 4, c, :, where] = value

    for c in range(5):
        if c == 3:
            pl.semaphore_wait(barrier, peers - 1)
            for d in range(1, peers):
                copy(d).start()
        for (face, half), value in layers(flow_ref, c).items():
            put(face, half, c, value)
        for (face, half), value in layers(adj_ref, c).items():
            put(face, half, 5 + c, value)
    for half in range(2):
        where = slice(half * LANES, (half + 1) * LANES)
        for ref, count in ((lat_ref, 4), (ver_ref, 2)):
            for face in range(count):
                prim = primitive([ref[face, c, :, where] for c in range(5)])
                for c in range(1, 5):
                    ref[face, c, :, where] = prim[c]
    own.wait()
    for d in range(1, peers):
        copy(d).wait()


def plan_kernel(capacity, owner_ref, link_ref, req_ref, place_ref, count_ref):
    def clear(p, carry):
        count_ref[p] = 0
        for s in range(capacity):
            req_ref[p, 0, s] = 0
        return carry

    lax.fori_loop(0, req_ref.shape[0], clear, 0)

    def ask(b, carry):
        for f in range(4):
            owner = owner_ref[f, 0, b]
            at = count_ref[owner]
            count_ref[owner] = at + 1
            req_ref[owner, 0, at] = link_ref[f, b] // 5 * 4 + (f ^ 1)
            place_ref[b * 4 + f] = owner * 4096 + at
        return carry

    lax.fori_loop(0, link_ref.shape[1], ask, 0)


def exchange_kernel(
    capacity, want_ref, lat_ref, ver_ref, ret_ref, low_ref, high_ref,
    stage, send_sem, recv_sem, up_sem, down_sem,
):
    peers = ret_ref.shape[0]
    me = lax.axis_index("blk")
    region = lax.axis_index("grp")
    last = lax.axis_size("grp") - 1
    has_low, has_high = region > 0, region < last

    def copy(d):
        peer = lax.rem(me + d, peers)
        return pltpu.make_async_remote_copy(
            src_ref=stage.at[peer],
            dst_ref=ret_ref.at[me],
            send_sem=send_sem.at[d],
            recv_sem=recv_sem.at[d],
            device_id={"blk": peer},
            device_id_type=MESH,
        )

    def vertical(source, target, sem, step):
        return pltpu.make_async_remote_copy(
            src_ref=ver_ref.at[source],
            dst_ref=target,
            send_sem=sem.at[0],
            recv_sem=sem.at[1],
            device_id={"grp": region + step},
            device_id_type=MESH,
        )

    upward = vertical(1, low_ref, up_sem, 1)
    downward = vertical(0, high_ref, down_sem, -1)
    barrier = pltpu.get_barrier_semaphore()
    for d in range(1, peers):
        pl.semaphore_signal(
            barrier, inc=1, device_id={"blk": lax.rem(me + d, peers)}, device_id_type=MESH
        )
    for there, step in ((has_low, -1), (has_high, 1)):
        @pl.when(there)
        def _():
            pl.semaphore_signal(
                barrier, inc=1, device_id={"grp": region + step}, device_id_type=MESH
            )

    def gather(peer, ref, at):
        def one(s, carry):
            code = want_ref[peer, 0, s]
            face, block = code & 3, code >> 2
            for c in range(10):
                ref[at, pl.ds(s * 10 + c, 1), :] = lat_ref[face, c, pl.ds(block, 1), :]
            return carry

        lax.fori_loop(0, capacity, one, 0)

    def fill(d):
        peer = lax.rem(me + d, peers)
        gather(peer, stage, peer)

    fill(1)
    pl.semaphore_wait(
        barrier, peers - 1 + has_low.astype(jnp.int32) + has_high.astype(jnp.int32)
    )

    def send(d, carry):
        fill(d)
        copy(d - 1).start()
        return carry

    lax.fori_loop(2, peers, send, 0)
    gather(me, ret_ref, me)
    copy(peers - 1).start()

    @pl.when(has_high)
    def _():
        upward.start()

    @pl.when(has_low)
    def _():
        downward.start()

    def far(ref):
        for c in range(10):
            ref[c] = jnp.full(ref.shape[1:], FREESTREAM[c] if c < 5 else 0.0, jnp.float32)

    @pl.when(has_low)
    def _():
        downward.wait_send()
        upward.wait_recv()

    @pl.when(jnp.logical_not(has_low))
    def _():
        far(low_ref)

    @pl.when(has_high)
    def _():
        upward.wait_send()
        downward.wait_recv()

    @pl.when(jnp.logical_not(has_high))
    def _():
        far(high_ref)

    def finish(d, carry):
        copy(d).wait()
        return carry

    lax.fori_loop(1, peers, finish, 0)


def minmod(a, b):
    return jnp.where(a * b > 0.0, jnp.where(jnp.abs(a) < jnp.abs(b), a, b), 0.0)


def derive(state):
    rho, u, v, w, p = state
    inv_root = lax.rsqrt(rho)
    root = rho * inv_root
    enth = (3.5 * p) * (inv_root * inv_root) + 0.5 * (u * u + v * v + w * w)
    return (rho, (u, v, w), p, enth, root, (root * u, root * v, root * w), root * enth)


def roe(left, right, n):
    rho_l, vel_l, p_l, h_l, root_l, rv_l, rh_l = left
    rho_r, vel_r, p_r, h_r, root_r, rv_r, rh_r = right
    t1, t2 = [a for a in range(3) if a != n]
    r = lax.rsqrt(root_l + root_r)
    inv = r * r
    vel = [(a + b) * inv for a, b in zip(rv_l, rv_r)]
    enth = (rh_l + rh_r) * inv
    half_sq = 0.5 * (vel[0] * vel[0] + vel[1] * vel[1] + vel[2] * vel[2])
    c_sq = 0.4 * (enth - half_sq)
    inv_c = lax.rsqrt(c_sq)
    c = c_sq * inv_c
    inv_c_sq = inv_c * inv_c
    rho = root_l * root_r
    un = vel[n]
    dp = p_r - p_l
    scaled = dp * inv_c_sq
    half = 0.5 * scaled
    jump = (0.5 * (rho * inv_c)) * (vel_r[n] - vel_l[n])
    spread, tenth, factor = 0.2 * c, 0.1 * c, 2.5 * inv_c

    def rate(x):
        x = jnp.abs(x)
        return jnp.where(x < spread, x * x * factor + tenth, x)

    slow = rate(un - c) * (half - jump)
    fast = rate(un + c) * (half + jump)
    speed = jnp.abs(un)
    mid = speed * ((rho_r - rho_l) - scaled)
    shear = speed * rho
    both = slow + fast
    diff = c * (fast - slow)
    mass = both + mid
    s1 = shear * (vel_r[t1] - vel_l[t1])
    s2 = shear * (vel_r[t2] - vel_l[t2])
    m_l, m_r = rho_l * vel_l[n], rho_r * vel_r[n]
    out = [None] * 5
    out[0] = m_l + m_r - mass
    out[1 + n] = m_l * vel_l[n] + m_r * vel_r[n] + (p_l + p_r) - (un * mass + diff)
    out[1 + t1] = m_l * vel_l[t1] + m_r * vel_r[t1] - (vel[t1] * mass + s1)
    out[1 + t2] = m_l * vel_l[t2] + m_r * vel_r[t2] - (vel[t2] * mass + s2)
    out[4] = (
        m_l * h_l + m_r * h_r
        - (enth * both + un * diff + mid * half_sq + vel[t1] * s1 + vel[t2] * s2)
    )
    return out


def quads(base, q1, q2):
    low = [b - q for b, q in zip(base, q1)]
    high = [b + q for b, q in zip(base, q1)]
    return [
        derive([b - q for b, q in zip(low, q2)]),
        derive([b + q for b, q in zip(low, q2)]),
        derive([b - q for b, q in zip(high, q2)]),
        derive([b + q for b, q in zip(high, q2)]),
    ]


def moments(lefts, rights, n):
    f = [roe(a, b, n) for a, b in zip(lefts, rights)]
    zero, first, second = [], [], []
    for c in range(5):
        low, high = f[0][c] + f[1][c], f[2][c] + f[3][c]
        zero.append(low + high)
        first.append(high - low)
        second.append((f[1][c] - f[0][c]) + (f[3][c] - f[2][c]))
    return zero + first + second


def dot(a, b):
    total = a[0] * b[0]
    for x, y in zip(a[1:], b[1:]):
        total = total + x * y
    return total


def main_kernel(
    place_ref, link_ref, ver_link_ref,
    flow_ref, adj_ref, flag_ref, ret_ref, low_ref, high_ref,
    out_ref,
    val, slope, solid, ghost, low_k, low_j, mom_k, mom_j, mom_i, lo_solid,
):
    blocks = flow_ref.shape[1]
    groups = blocks // PACK
    lane = iota((8, LANES), 1)
    row = iota((8, LANES), 0)
    top = row < PACK
    slot, spot = lane >> 4, lane & 15

    def pack(parts):
        tiles = []
        for g in range(groups):
            at = g * PACK % 8
            first, second = parts[g * PACK // 8]
            if first.shape[0] == PACK:
                tiles.append(jnp.concatenate([first, second], axis=0))
            elif at == 0:
                tiles.append(jnp.where(top, first, pltpu.roll(second, 4, 0)))
            else:
                tiles.append(jnp.where(top, pltpu.roll(first, 4, 0), second))
        return tiles

    def read(load, i):
        parts = []
        for start in range(0, blocks, 8):
            rows = slice(start, min(start + 8, blocks))
            parts.append(
                [load(rows, pl.ds(pl.multiple_of(i * PLANE + h * LANES, LANES), LANES)) for h in range(2)]
            )
        return pack(parts)

    def load_layer(i, carry):
        flow = [read(lambda r, s: flow_ref[c, r, s], i) for c in range(5)]
        for g in range(groups):
            for c, x in enumerate(primitive([f[g] for f in flow])):
                val[g, c, 1 + i] = x
        for c in range(5):
            for g, x in enumerate(read(lambda r, s: adj_ref[c, r, s], i)):
                val[g, 5 + c, 1 + i] = x
        for g, x in enumerate(read(lambda r, s: flag_ref[r, s], i)):
            solid[g, 1 + i] = x.astype(jnp.float32)
        return carry

    lax.fori_loop(0, EDGE, load_layer, 0)

    def load_ghost(c, carry):
        for b in range(blocks):
            g, at = b // PACK, b % PACK
            for f in range(6):
                if f < 4:
                    at_row = place_ref[b * 4 + f]
                    x = ret_ref[at_row >> 12, pl.ds((at_row & 4095) * 10 + c, 1), :]
                else:
                    ref = low_ref if f == 4 else high_ref
                    x = ref[c, pl.ds(ver_link_ref[f - 4, b] // 5, 1), :]
                ghost[g, f, c, at : at + 1, :] = x[:, :LANES]
                ghost[g, f, c, PACK + at : PACK + at + 1, :] = x[:, LANES:]
        return carry

    lax.fori_loop(0, 10, load_ghost, 0)
    upper_half = 1 - (row >> 2)
    for g in range(groups):
        for f in range(6):
            code = 0
            for at in range(PACK):
                b = g * PACK + at
                one = lax.rem(link_ref[f, b] if f < 4 else ver_link_ref[f - 4, b], 5)
                if f >= 4:
                    one = jnp.where(one == 4, 4, ((one & 1) << 1) + (one >> 1))
                code = jnp.where((row & 3) == at, one, code)
            half = 1 - upper_half
            own = (code == 4) | ((code >> 1) == half)
            quarter = ((4 * half + (slot >> 1)) << 4) + ((code & 1) << 3) + (spot >> 1)
            index = jnp.where(code == 4, lane, quarter)
            for c in range(10):
                x = ghost[g, f, c]
                x = jnp.where(own, x, pltpu.roll(x, 4, 0))
                x = jnp.take_along_axis(x, index, axis=1, mode="promise_in_bounds")
                ghost[g, f, c] = x
    for g in range(groups):
        nothing = jnp.zeros((8, LANES), jnp.float32)
        solid[g, 0] = nothing
        solid[g, EDGE + 1] = nothing
        for c in range(10):
            val[g, c, 0] = ghost[g, 0, c]
            val[g, c, EDGE + 1] = ghost[g, 1, c]
    for d in range(3):
        for c in range(5):
            nothing = jnp.zeros((8, LANES), jnp.float32)
            slope[d, c, 0] = nothing
            slope[d, c, EDGE + 1] = nothing

    def next_k(x, edge, i):
        edge = 0.0 if edge is None else pltpu.roll(edge, 15 - i, 1)
        return jnp.where(spot == 15, edge, pltpu.roll(x, LANES - 1, 1))

    def prev_k(x, edge, i):
        edge = 0.0 if edge is None else pltpu.roll(edge, (LANES - i) % LANES, 1)
        return jnp.where(spot == 0, edge, pltpu.roll(x, 1, 1))

    def place(edge, i, lane_at, upper):
        if edge is None:
            return 0.0
        edge = pltpu.roll(edge, (2 * LANES + lane_at - (i & 7) * 16) % LANES, 1)
        same = (i >> 3) == (1 if upper else 0)
        return jnp.where(same, edge, pltpu.roll(edge, 4, 0))

    def next_j(x, edge, i):
        y = pltpu.roll(x, LANES - 16, 1)
        z = jnp.where(top, pltpu.roll(y, 4, 0), place(edge, i, LANES - 16, True))
        return jnp.where(slot == 7, z, y)

    def prev_j(x, edge, i):
        y = pltpu.roll(x, 16, 1)
        z = jnp.where(top, place(edge, i, 0, False), pltpu.roll(y, 4, 0))
        return jnp.where(slot == 0, z, y)

    def group(g, carry):
        def slopes(i, inner):
            at_k = spot == i
            at_j = ((row >> 2) == (i >> 3)) & (slot == (i & 7))
            for c in range(10):
                own = val[g, c, 1 + i]
                found = [
                    minmod(val[g, c, 2 + i] - own, own - val[g, c, i]),
                    minmod(next_j(own, ghost[g, 3, c], i) - own, own - prev_j(own, ghost[g, 2, c], i)),
                    minmod(next_k(own, ghost[g, 5, c], i) - own, own - prev_k(own, ghost[g, 4, c], i)),
                ]
                found = [0.25 * s for s in found]
                for d in range(3):
                    slope[d, c, 1 + i] = found[d]
                if c < 5:
                    for d, x in enumerate([own, *found]):
                        low_k[d, c] = jnp.where(at_k, pltpu.roll(x, i, 1), low_k[d, c])
                        x = jnp.where(top, x, pltpu.roll(x, 4, 0))
                        low_j[d, c] = jnp.where(at_j, pltpu.roll(x, (i & 7) * 16, 1), low_j[d, c])
            return inner

        lax.fori_loop(0, EDGE, slopes, 0)

        def first_faces(n, lower, cell):
            t1, t2 = [a for a in range(3) if a != n]
            left = derive(lower)
            base = [cell(0, c) - cell(1 + n, c) for c in range(5)]
            rights = quads(base, [cell(1 + t1, c) for c in range(5)], [cell(1 + t2, c) for c in range(5)])
            return moments([left] * 4, rights, n)

        for ref, n in ((mom_j, 1), (mom_k, 2)):
            source = low_j if n == 1 else low_k
            found = first_faces(n, [ghost[g, 2 * n, c] for c in range(5)], lambda d, c: source[d, c])
            for c in range(15):
                ref[c] = found[c]
        found = first_faces(
            0,
            [ghost[g, 0, c] for c in range(5)],
            lambda d, c: val[g, c, 1] if d == 0 else slope[d - 1, c, 1],
        )
        for c in range(15):
            mom_i[c] = found[c]

        def layer(i, inner):
            v = [val[g, c, 1 + i] for c in range(5)]
            q = [[slope[d, c, 1 + i] for c in range(5)] for d in range(3)]
            av = [val[g, 5 + c, 1 + i] for c in range(5)]
            aq = [[slope[d, 5 + c, 1 + i] for c in range(5)] for d in range(3)]
            child = {}
            for a in range(2):
                base = [x + y if a else x - y for x, y in zip(v, q[0])]
                for at, state in enumerate(quads(base, q[1], q[2])):
                    child[a, at >> 1, at & 1] = state

            def side(n, high):
                order = [(s, t) for s in range(2) for t in range(2)]
                return [child[tuple([*st[:n], high, *st[n:]])] for st in order]

            own_solid = solid[g, 1 + i]
            total = jnp.zeros((8, LANES), jnp.float32)
            for n in range(3):
                t1, t2 = [a for a in range(3) if a != n]
                f = [roe(a, b, n) for a, b in zip(side(n, 0), side(n, 1))]
                inside = [(f[0][c] + f[1][c]) + (f[2][c] + f[3][c]) for c in range(5)]
                total = total - 2.0 * dot(aq[n], inside)
                if n == 0:
                    base = [val[g, c, 2 + i] - slope[0, c, 2 + i] for c in range(5)]
                    q1 = [slope[1, c, 2 + i] for c in range(5)]
                    q2 = [slope[2, c, 2 + i] for c in range(5)]
                    up_solid, down_solid = solid[g, 2 + i], solid[g, i]
                else:
                    ahead, behind = (next_j, prev_j) if n == 1 else (next_k, prev_k)
                    base = [ahead(v[c] - q[n][c], ghost[g, 2 * n + 1, c], i) for c in range(5)]
                    q1 = [ahead(q[t1][c], None, i) for c in range(5)]
                    q2 = [ahead(q[t2][c], None, i) for c in range(5)]
                    up_solid, down_solid = ahead(own_solid, None, i), behind(own_solid, None, i)
                above = moments(side(n, 1), quads(base, q1, q2), n)
                if n == 0:
                    below = [mom_i[c] for c in range(15)]
                    for c in range(15):
                        mom_i[c] = above[c]
                else:
                    first = mom_j if n == 1 else mom_k
                    below = [behind(above[c], first[c], i) for c in range(15)]
                outer = [x + y for x, y in zip(av, aq[n])]
                inner_side = [x - y for x, y in zip(av, aq[n])]
                upper = dot([*outer, *aq[t1], *aq[t2]], above)
                lower = dot([*inner_side, *aq[t1], *aq[t2]], below)
                cross = aq[t1][1 + n] * q[t1][4] + aq[t2][1 + n] * q[t2][4]
                wall_up = 8.0 * (outer[1 + n] * (v[4] + q[n][4]) + cross)
                wall_down = 8.0 * (inner_side[1 + n] * (v[4] - q[n][4]) + cross)
                total = total + (
                    jnp.where(up_solid > 0.5, wall_up, upper)
                    - jnp.where(down_solid > 0.5, wall_down, lower)
                )
            total = jnp.where(own_solid > 0.5, 0.0, 0.5 * jnp.abs(total))
            lo_solid[g, i] = total
            return inner

        lax.fori_loop(0, EDGE, layer, 0)
        return carry

    lax.fori_loop(0, groups, group, 0)

    def store(i, carry):
        for g in range(groups):
            x = lo_solid[g, i]
            for h in range(2):
                out_ref[
                    g * PACK : (g + 1) * PACK,
                    pl.ds(pl.multiple_of(i * PLANE + h * LANES, LANES), LANES),
                ] = x[h * PACK : (h + 1) * PACK]
        return carry

    lax.fori_loop(0, EDGE, store, 0)


def local(flow, adjoint, cut_flag, lateral_owner, lateral_link, vertical_link):
    blocks = flow.shape[0]
    groups = blocks // PACK
    peers = lax.axis_size("blk")
    capacity = max(2, 6 * blocks // peers)
    flow_t = jnp.transpose(flow, (1, 0, 2))
    adj_t = jnp.transpose(adjoint, (1, 0, 2))
    f32 = functools.partial(jax.ShapeDtypeStruct, dtype=jnp.float32)

    owner_t = jnp.transpose(lateral_owner, (1, 2, 0))
    link_t, ver_link_t = lateral_link.T, vertical_link.T
    i32 = functools.partial(jax.ShapeDtypeStruct, dtype=jnp.int32)
    requests, place = pl.pallas_call(
        functools.partial(plan_kernel, capacity),
        out_shape=(i32((peers, 1, LANES)), i32((blocks * 4,))),
        in_specs=[SMEM, SMEM],
        out_specs=(SMEM, SMEM),
        scratch_shapes=[pltpu.SMEM((peers,), jnp.int32)],
        name="plan",
    )(owner_t, link_t)

    lateral, vertical, wanted = pl.pallas_call(
        faces_kernel,
        out_shape=(
            f32((4, 10, blocks, PLANE)),
            f32((2, 10, blocks, PLANE)),
            i32((peers, 1, LANES)),
        ),
        in_specs=[VMEM] * 3,
        out_specs=(VMEM,) * 3,
        scratch_shapes=[
            pltpu.SemaphoreType.DMA((peers,)),
            pltpu.SemaphoreType.DMA((peers,)),
            pltpu.SemaphoreType.DMA,
        ],
        compiler_params=pltpu.CompilerParams(collective_id=0, has_side_effects=True),
        name="faces",
    )(requests, flow_t, adj_t)

    returned, from_low, from_high = pl.pallas_call(
        functools.partial(exchange_kernel, capacity),
        out_shape=(
            f32((peers, capacity * 10, PLANE)),
            f32((10, blocks, PLANE)),
            f32((10, blocks, PLANE)),
        ),
        in_specs=[SMEM, VMEM, VMEM],
        out_specs=(VMEM,) * 3,
        scratch_shapes=[
            pltpu.VMEM((peers, capacity * 10, PLANE), jnp.float32),
            pltpu.SemaphoreType.DMA((peers,)),
            pltpu.SemaphoreType.DMA((peers,)),
            pltpu.SemaphoreType.DMA((2,)),
            pltpu.SemaphoreType.DMA((2,)),
        ],
        compiler_params=pltpu.CompilerParams(collective_id=1, has_side_effects=True),
        name="exchange",
    )(wanted, lateral, vertical)

    tile = functools.partial(pltpu.VMEM, dtype=jnp.float32)
    return pl.pallas_call(
        main_kernel,
        out_shape=f32((blocks, EDGE * PLANE)),
        in_specs=[SMEM] * 3 + [VMEM] * 6,
        out_specs=VMEM,
        scratch_shapes=[
            tile((groups, 10, EDGE + 2, 8, LANES)),
            tile((3, 10, EDGE + 2, 8, LANES)),
            tile((groups, EDGE + 2, 8, LANES)),
            tile((groups, 6, 10, 8, LANES)),
            tile((4, 5, 8, LANES)),
            tile((4, 5, 8, LANES)),
            tile((15, 8, LANES)),
            tile((15, 8, LANES)),
            tile((15, 8, LANES)),
            tile((groups, EDGE, 8, LANES)),
        ],
        compiler_params=pltpu.CompilerParams(vmem_limit_bytes=50 * 1024 * 1024),
        name="indicator",
    )(
        place, link_t, ver_link_t,
        flow_t, adj_t, cut_flag, returned, from_low, from_high,
    )


def solution(mesh):
    spec3 = P(("blk", "grp"), None, None)
    spec2 = P(("blk", "grp"), None)
    return jax.shard_map(
        local,
        mesh=mesh,
        in_specs=(spec3, spec3, spec2, spec3, spec2, spec2),
        out_specs=spec2,
        check_vma=False,
    )
```

```python
import functools

import jax
import jax.numpy as jnp
from jax import lax
from jax.experimental import pallas as pl
from jax.experimental.pallas import tpu as pltpu
from jax.sharding import PartitionSpec as P

EDGE = 16
PLANE = EDGE * EDGE
LANES = 128
PACK = 4
FREESTREAM = (1.0, 0.0, 0.0, 0.3, 1.0)
VMEM = pl.BlockSpec(memory_space=pltpu.VMEM)
SMEM = pl.BlockSpec(memory_space=pltpu.SMEM)
HBM = pl.BlockSpec(memory_space=pltpu.HBM)
MESH = pl.DeviceIdType.MESH


def iota(shape, dim):
    return lax.broadcasted_iota(jnp.int32, shape, dim)


def primitive(state):
    density, mom, energy = state[0], state[1:4], state[4]
    root = lax.rsqrt(density)
    inverse = root * root
    vel = [m * inverse for m in mom]
    square = vel[0] * vel[0] + vel[1] * vel[1] + vel[2] * vel[2]
    return [density, *vel, 0.4 * (energy - 0.5 * density * square)]


def halo_kernel(
    capacity, req_ref, flow_ref, adj_ref, ret_ref, low_ref, high_ref,
    lat_ref, ver_ref, want_ref, index_ref, stage,
    ask_sem, asked_sem, send_sem, recv_sem, up_sem, down_sem, own_sem,
):
    blocks = flow_ref.shape[1]
    peers = req_ref.shape[0]
    me = lax.axis_index("blk")

    def request(d):
        peer = lax.rem(me + d, peers)
        return pltpu.make_async_remote_copy(
            src_ref=req_ref.at[peer],
            dst_ref=want_ref.at[me],
            send_sem=ask_sem.at[d],
            recv_sem=asked_sem.at[d],
            device_id={"blk": peer},
            device_id_type=MESH,
        )

    barrier = pltpu.get_barrier_semaphore()
    for d in range(1, peers):
        pl.semaphore_signal(
            barrier, inc=1, device_id={"blk": lax.rem(me + d, peers)}, device_id_type=MESH
        )
    region = lax.axis_index("grp")
    last = lax.axis_size("grp") - 1
    has_low, has_high = region > 0, region < last
    for there, step in ((has_low, -1), (has_high, 1)):
        @pl.when(there)
        def _():
            pl.semaphore_signal(
                barrier, inc=1, device_id={"grp": region + step}, device_id_type=MESH
            )
    own = pltpu.make_async_copy(req_ref.at[me], want_ref.at[me], own_sem)
    own.start()
    lane = iota((blocks, LANES), 1)
    slot, spot = lane >> 4, lane & 15

    def layers(ref, c):
        def tile(i, half):
            return ref[c, :, i * PLANE + half * LANES : i * PLANE + (half + 1) * LANES]

        out = {}
        for half in range(2):
            out[0, half] = tile(0, half)
            out[1, half] = tile(EDGE - 1, half)
            low_j = high_j = low_k = high_k = jnp.zeros((blocks, LANES), jnp.float32)
            for i in range(EDGE):
                if i // 8 == half:
                    il = i % 8
                    low_j = jnp.where(slot == il, pltpu.roll(tile(i, 0), il * 16, 1), low_j)
                    high_j = jnp.where(
                        slot == il, pltpu.roll(tile(i, 1), (il * 16 + 16) % LANES, 1), high_j
                    )
                here = tile(i, half)
                low_k = jnp.where(spot == i, pltpu.roll(here, i, 1), low_k)
                high_k = jnp.where(spot == i, pltpu.roll(here, (LANES + i - 15) % LANES, 1), high_k)
            out[2, half], out[3, half], out[4, half], out[5, half] = low_j, high_j, low_k, high_k
        return out

    def put(face, half, c, value):
        where = slice(half * LANES, (half + 1) * LANES)
        if face < 4:
            lat_ref[face, c, :, where] = value
        else:
            ver_ref[face - 4, c, :, where] = value

    for c in range(5):
        if c == 3:
            pl.semaphore_wait(
                barrier, peers - 1 + has_low.astype(jnp.int32) + has_high.astype(jnp.int32)
            )
            for d in range(1, peers):
                request(d).start()
        for (face, half), value in layers(flow_ref, c).items():
            put(face, half, c, value)
        for (face, half), value in layers(adj_ref, c).items():
            put(face, half, 5 + c, value)
    for half in range(2):
        where = slice(half * LANES, (half + 1) * LANES)
        for ref, count in ((lat_ref, 4), (ver_ref, 2)):
            for face in range(count):
                prim = primitive([ref[face, c, :, where] for c in range(5)])
                for c in range(1, 5):
                    ref[face, c, :, where] = prim[c]
    own.wait()
    for d in range(1, peers):
        request(d).wait()
    indices = pltpu.make_async_copy(want_ref, index_ref, own_sem)
    indices.start()
    indices.wait()
    def copy(d):
        peer = lax.rem(me + d, peers)
        return pltpu.make_async_remote_copy(
            src_ref=stage.at[peer],
            dst_ref=ret_ref.at[me],
            send_sem=send_sem.at[d],
            recv_sem=recv_sem.at[d],
            device_id={"blk": peer},
            device_id_type=MESH,
        )

    def vertical(source, target, sem, step):
        return pltpu.make_async_remote_copy(
            src_ref=ver_ref.at[source],
            dst_ref=target,
            send_sem=sem.at[0],
            recv_sem=sem.at[1],
            device_id={"grp": region + step},
            device_id_type=MESH,
        )

    upward = vertical(1, low_ref, up_sem, 1)
    downward = vertical(0, high_ref, down_sem, -1)
    def gather(peer, ref, at):
        def one(s, carry):
            code = index_ref[peer, 0, s]
            face, block = code & 3, code >> 2
            for c in range(10):
                ref[at, pl.ds(s * 10 + c, 1), :] = lat_ref[face, c, pl.ds(block, 1), :]
            return carry

        lax.fori_loop(0, capacity, one, 0)

    def fill(d):
        peer = lax.rem(me + d, peers)
        gather(peer, stage, peer)

    fill(1)

    @pl.when(has_high)
    def _():
        upward.start()

    @pl.when(has_low)
    def _():
        downward.start()

    def send(d, carry):
        fill(d)
        copy(d - 1).start()
        return carry

    lax.fori_loop(2, peers, send, 0)
    gather(me, stage, me)
    copy(peers - 1).start()

    def far(ref):
        for c in range(10):
            ref[c] = jnp.full(ref.shape[1:], FREESTREAM[c] if c < 5 else 0.0, jnp.float32)

    mine = pltpu.make_async_copy(stage.at[me], ret_ref.at[me], own_sem)
    mine.start()

    @pl.when(has_low)
    def _():
        downward.wait_send()
        upward.wait_recv()

    @pl.when(jnp.logical_not(has_low))
    def _():
        far(low_ref)

    @pl.when(has_high)
    def _():
        upward.wait_send()
        downward.wait_recv()

    @pl.when(jnp.logical_not(has_high))
    def _():
        far(high_ref)

    def finish(d, carry):
        copy(d).wait()
        return carry

    lax.fori_loop(1, peers, finish, 0)
    mine.wait()


def plan_kernel(capacity, owner_ref, link_ref, req_ref, place_ref, count_ref):
    def clear(p, carry):
        count_ref[p] = 0
        for s in range(capacity):
            req_ref[p, 0, s] = 0
        return carry

    lax.fori_loop(0, req_ref.shape[0], clear, 0)

    def ask(b, carry):
        for f in range(4):
            owner = owner_ref[f, 0, b]
            at = count_ref[owner]
            count_ref[owner] = at + 1
            req_ref[owner, 0, at] = link_ref[f, b] // 5 * 4 + (f ^ 1)
            place_ref[b * 4 + f] = owner * 4096 + at
        return carry

    lax.fori_loop(0, link_ref.shape[1], ask, 0)


def minmod(a, b):
    return jnp.where(a * b > 0.0, jnp.where(jnp.abs(a) < jnp.abs(b), a, b), 0.0)


def derive(state):
    rho, u, v, w, p = state
    inv_root = lax.rsqrt(rho)
    root = rho * inv_root
    enth = (3.5 * p) * (inv_root * inv_root) + 0.5 * (u * u + v * v + w * w)
    return (rho, (u, v, w), p, enth, root, (root * u, root * v, root * w), root * enth)


def roe(left, right, n):
    rho_l, vel_l, p_l, h_l, root_l, rv_l, rh_l = left
    rho_r, vel_r, p_r, h_r, root_r, rv_r, rh_r = right
    t1, t2 = [a for a in range(3) if a != n]
    r = lax.rsqrt(root_l + root_r)
    inv = r * r
    vel = [(a + b) * inv for a, b in zip(rv_l, rv_r)]
    enth = (rh_l + rh_r) * inv
    half_sq = 0.5 * (vel[0] * vel[0] + vel[1] * vel[1] + vel[2] * vel[2])
    c_sq = 0.4 * (enth - half_sq)
    inv_c = lax.rsqrt(c_sq)
    c = c_sq * inv_c
    inv_c_sq = inv_c * inv_c
    rho = root_l * root_r
    un = vel[n]
    dp = p_r - p_l
    scaled = dp * inv_c_sq
    half = 0.5 * scaled
    jump = (0.5 * (rho * inv_c)) * (vel_r[n] - vel_l[n])
    spread, tenth, factor = 0.2 * c, 0.1 * c, 2.5 * inv_c

    def rate(x):
        x = jnp.abs(x)
        return jnp.where(x < spread, x * x * factor + tenth, x)

    slow = rate(un - c) * (half - jump)
    fast = rate(un + c) * (half + jump)
    speed = jnp.abs(un)
    mid = speed * ((rho_r - rho_l) - scaled)
    shear = speed * rho
    both = slow + fast
    diff = c * (fast - slow)
    mass = both + mid
    s1 = shear * (vel_r[t1] - vel_l[t1])
    s2 = shear * (vel_r[t2] - vel_l[t2])
    m_l, m_r = rho_l * vel_l[n], rho_r * vel_r[n]
    out = [None] * 5
    out[0] = m_l + m_r - mass
    out[1 + n] = m_l * vel_l[n] + m_r * vel_r[n] + (p_l + p_r) - (un * mass + diff)
    out[1 + t1] = m_l * vel_l[t1] + m_r * vel_r[t1] - (vel[t1] * mass + s1)
    out[1 + t2] = m_l * vel_l[t2] + m_r * vel_r[t2] - (vel[t2] * mass + s2)
    out[4] = (
        m_l * h_l + m_r * h_r
        - (enth * both + un * diff + mid * half_sq + vel[t1] * s1 + vel[t2] * s2)
    )
    return out


def quads(base, q1, q2):
    low = [b - q for b, q in zip(base, q1)]
    high = [b + q for b, q in zip(base, q1)]
    return [
        derive([b - q for b, q in zip(low, q2)]),
        derive([b + q for b, q in zip(low, q2)]),
        derive([b - q for b, q in zip(high, q2)]),
        derive([b + q for b, q in zip(high, q2)]),
    ]


def moments(lefts, rights, n):
    f = [roe(a, b, n) for a, b in zip(lefts, rights)]
    zero, first, second = [], [], []
    for c in range(5):
        low, high = f[0][c] + f[1][c], f[2][c] + f[3][c]
        zero.append(low + high)
        first.append(high - low)
        second.append((f[1][c] - f[0][c]) + (f[3][c] - f[2][c]))
    return zero + first + second


def dot(a, b):
    total = a[0] * b[0]
    for x, y in zip(a[1:], b[1:]):
        total = total + x * y
    return total


def main_kernel(
    place_ref, link_ref, ver_link_ref,
    flow_ref, adj_ref, flag_ref, ret_hbm, low_hbm, high_hbm,
    out_ref,
    ret_ref, low_ref, high_ref, sems,
    val, slope, solid, ghost, low_k, low_j, mom_k, mom_j, mom_i, lo_solid,
):
    blocks = flow_ref.shape[1]
    groups = blocks // PACK
    lane = iota((8, LANES), 1)
    row = iota((8, LANES), 0)
    top = row < PACK
    slot, spot = lane >> 4, lane & 15

    def pack(parts):
        tiles = []
        for g in range(groups):
            at = g * PACK % 8
            first, second = parts[g * PACK // 8]
            if first.shape[0] == PACK:
                tiles.append(jnp.concatenate([first, second], axis=0))
            elif at == 0:
                tiles.append(jnp.where(top, first, pltpu.roll(second, 4, 0)))
            else:
                tiles.append(jnp.where(top, pltpu.roll(first, 4, 0), second))
        return tiles

    def read(load, i):
        parts = []
        for start in range(0, blocks, 8):
            rows = slice(start, min(start + 8, blocks))
            parts.append(
                [load(rows, pl.ds(pl.multiple_of(i * PLANE + h * LANES, LANES), LANES)) for h in range(2)]
            )
        return pack(parts)

    def load_layer(i, carry):
        flow = [read(lambda r, s: flow_ref[c, r, s], i) for c in range(5)]
        for g in range(groups):
            for c, x in enumerate(primitive([f[g] for f in flow])):
                val[g, c, 1 + i] = x
        for c in range(5):
            for g, x in enumerate(read(lambda r, s: adj_ref[c, r, s], i)):
                val[g, 5 + c, 1 + i] = x
        for g, x in enumerate(read(lambda r, s: flag_ref[r, s], i)):
            solid[g, 1 + i] = x.astype(jnp.float32)
        return carry

    pairs = ((ret_hbm, ret_ref), (low_hbm, low_ref), (high_hbm, high_ref))
    copies = [pltpu.make_async_copy(a, b, sems.at[at]) for at, (a, b) in enumerate(pairs)]
    for copy in copies:
        copy.start()
    lax.fori_loop(0, EDGE, load_layer, 0)
    for copy in copies:
        copy.wait()

    def load_ghost(c, carry):
        for b in range(blocks):
            g, at = b // PACK, b % PACK
            for f in range(6):
                if f < 4:
                    at_row = place_ref[b * 4 + f]
                    x = ret_ref[at_row >> 12, pl.ds((at_row & 4095) * 10 + c, 1), :]
                else:
                    ref = low_ref if f == 4 else high_ref
                    x = ref[c, pl.ds(ver_link_ref[f - 4, b] // 5, 1), :]
                ghost[g, f, c, at : at + 1, :] = x[:, :LANES]
                ghost[g, f, c, PACK + at : PACK + at + 1, :] = x[:, LANES:]
        return carry

    lax.fori_loop(0, 10, load_ghost, 0)
    upper_half = 1 - (row >> 2)
    for g in range(groups):
        for f in range(6):
            code = 0
            for at in range(PACK):
                b = g * PACK + at
                one = lax.rem(link_ref[f, b] if f < 4 else ver_link_ref[f - 4, b], 5)
                if f >= 4:
                    one = jnp.where(one == 4, 4, ((one & 1) << 1) + (one >> 1))
                code = jnp.where((row & 3) == at, one, code)
            half = 1 - upper_half
            own = (code == 4) | ((code >> 1) == half)
            quarter = ((4 * half + (slot >> 1)) << 4) + ((code & 1) << 3) + (spot >> 1)
            index = jnp.where(code == 4, lane, quarter)
            for c in range(10):
                x = ghost[g, f, c]
                x = jnp.where(own, x, pltpu.roll(x, 4, 0))
                x = jnp.take_along_axis(x, index, axis=1, mode="promise_in_bounds")
                ghost[g, f, c] = x
    for g in range(groups):
        nothing = jnp.zeros((8, LANES), jnp.float32)
        solid[g, 0] = nothing
        solid[g, EDGE + 1] = nothing
        for c in range(10):
            val[g, c, 0] = ghost[g, 0, c]
            val[g, c, EDGE + 1] = ghost[g, 1, c]
    for d in range(3):
        for c in range(5):
            nothing = jnp.zeros((8, LANES), jnp.float32)
            slope[d, c, 0] = nothing
            slope[d, c, EDGE + 1] = nothing

    def next_k(x, edge, i):
        edge = 0.0 if edge is None else pltpu.roll(edge, 15 - i, 1)
        return jnp.where(spot == 15, edge, pltpu.roll(x, LANES - 1, 1))

    def prev_k(x, edge, i):
        edge = 0.0 if edge is None else pltpu.roll(edge, (LANES - i) % LANES, 1)
        return jnp.where(spot == 0, edge, pltpu.roll(x, 1, 1))

    def place(edge, i, lane_at, upper):
        if edge is None:
            return 0.0
        edge = pltpu.roll(edge, (2 * LANES + lane_at - (i & 7) * 16) % LANES, 1)
        same = (i >> 3) == (1 if upper else 0)
        return jnp.where(same, edge, pltpu.roll(edge, 4, 0))

    def next_j(x, edge, i):
        y = pltpu.roll(x, LANES - 16, 1)
        z = jnp.where(top, pltpu.roll(y, 4, 0), place(edge, i, LANES - 16, True))
        return jnp.where(slot == 7, z, y)

    def prev_j(x, edge, i):
        y = pltpu.roll(x, 16, 1)
        z = jnp.where(top, place(edge, i, 0, False), pltpu.roll(y, 4, 0))
        return jnp.where(slot == 0, z, y)

    def group(g, carry):
        def slopes(i, inner):
            at_k = spot == i
            at_j = ((row >> 2) == (i >> 3)) & (slot == (i & 7))
            for c in range(10):
                own = val[g, c, 1 + i]
                found = [
                    minmod(val[g, c, 2 + i] - own, own - val[g, c, i]),
                    minmod(next_j(own, ghost[g, 3, c], i) - own, own - prev_j(own, ghost[g, 2, c], i)),
                    minmod(next_k(own, ghost[g, 5, c], i) - own, own - prev_k(own, ghost[g, 4, c], i)),
                ]
                found = [0.25 * s for s in found]
                for d in range(3):
                    slope[d, c, 1 + i] = found[d]
                if c < 5:
                    for d, x in enumerate([own, *found]):
                        low_k[d, c] = jnp.where(at_k, pltpu.roll(x, i, 1), low_k[d, c])
                        x = jnp.where(top, x, pltpu.roll(x, 4, 0))
                        low_j[d, c] = jnp.where(at_j, pltpu.roll(x, (i & 7) * 16, 1), low_j[d, c])
            return inner

        lax.fori_loop(0, EDGE, slopes, 0)

        def first_faces(n, lower, cell):
            t1, t2 = [a for a in range(3) if a != n]
            left = derive(lower)
            base = [cell(0, c) - cell(1 + n, c) for c in range(5)]
            rights = quads(base, [cell(1 + t1, c) for c in range(5)], [cell(1 + t2, c) for c in range(5)])
            return moments([left] * 4, rights, n)

        for ref, n in ((mom_j, 1), (mom_k, 2)):
            source = low_j if n == 1 else low_k
            found = first_faces(n, [ghost[g, 2 * n, c] for c in range(5)], lambda d, c: source[d, c])
            for c in range(15):
                ref[c] = found[c]
        found = first_faces(
            0,
            [ghost[g, 0, c] for c in range(5)],
            lambda d, c: val[g, c, 1] if d == 0 else slope[d - 1, c, 1],
        )
        for c in range(15):
            mom_i[c] = found[c]

        def layer(i, inner):
            v = [val[g, c, 1 + i] for c in range(5)]
            q = [[slope[d, c, 1 + i] for c in range(5)] for d in range(3)]
            av = [val[g, 5 + c, 1 + i] for c in range(5)]
            aq = [[slope[d, 5 + c, 1 + i] for c in range(5)] for d in range(3)]
            child = {}
            for a in range(2):
                base = [x + y if a else x - y for x, y in zip(v, q[0])]
                for at, state in enumerate(quads(base, q[1], q[2])):
                    child[a, at >> 1, at & 1] = state

            def side(n, high):
                order = [(s, t) for s in range(2) for t in range(2)]
                return [child[tuple([*st[:n], high, *st[n:]])] for st in order]

            own_solid = solid[g, 1 + i]
            total = jnp.zeros((8, LANES), jnp.float32)
            for n in range(3):
                t1, t2 = [a for a in range(3) if a != n]
                f = [roe(a, b, n) for a, b in zip(side(n, 0), side(n, 1))]
                inside = [(f[0][c] + f[1][c]) + (f[2][c] + f[3][c]) for c in range(5)]
                total = total - 2.0 * dot(aq[n], inside)
                if n == 0:
                    base = [val[g, c, 2 + i] - slope[0, c, 2 + i] for c in range(5)]
                    q1 = [slope[1, c, 2 + i] for c in range(5)]
                    q2 = [slope[2, c, 2 + i] for c in range(5)]
                    up_solid, down_solid = solid[g, 2 + i], solid[g, i]
                else:
                    ahead, behind = (next_j, prev_j) if n == 1 else (next_k, prev_k)
                    base = [ahead(v[c] - q[n][c], ghost[g, 2 * n + 1, c], i) for c in range(5)]
                    q1 = [ahead(q[t1][c], None, i) for c in range(5)]
                    q2 = [ahead(q[t2][c], None, i) for c in range(5)]
                    up_solid, down_solid = ahead(own_solid, None, i), behind(own_solid, None, i)
                above = moments(side(n, 1), quads(base, q1, q2), n)
                if n == 0:
                    below = [mom_i[c] for c in range(15)]
                    for c in range(15):
                        mom_i[c] = above[c]
                else:
                    first = mom_j if n == 1 else mom_k
                    below = [behind(above[c], first[c], i) for c in range(15)]
                outer = [x + y for x, y in zip(av, aq[n])]
                inner_side = [x - y for x, y in zip(av, aq[n])]
                upper = dot([*outer, *aq[t1], *aq[t2]], above)
                lower = dot([*inner_side, *aq[t1], *aq[t2]], below)
                cross = aq[t1][1 + n] * q[t1][4] + aq[t2][1 + n] * q[t2][4]
                wall_up = 8.0 * (outer[1 + n] * (v[4] + q[n][4]) + cross)
                wall_down = 8.0 * (inner_side[1 + n] * (v[4] - q[n][4]) + cross)
                total = total + (
                    jnp.where(up_solid > 0.5, wall_up, upper)
                    - jnp.where(down_solid > 0.5, wall_down, lower)
                )
            total = jnp.where(own_solid > 0.5, 0.0, 0.5 * jnp.abs(total))
            lo_solid[g, i] = total
            return inner

        lax.fori_loop(0, EDGE, layer, 0)
        return carry

    lax.fori_loop(0, groups, group, 0)

    def store(i, carry):
        for g in range(groups):
            x = lo_solid[g, i]
            for h in range(2):
                out_ref[
                    g * PACK : (g + 1) * PACK,
                    pl.ds(pl.multiple_of(i * PLANE + h * LANES, LANES), LANES),
                ] = x[h * PACK : (h + 1) * PACK]
        return carry

    lax.fori_loop(0, EDGE, store, 0)


def local(flow, adjoint, cut_flag, lateral_owner, lateral_link, vertical_link):
    blocks = flow.shape[0]
    groups = blocks // PACK
    peers = lax.axis_size("blk")
    capacity = max(2, 6 * blocks // peers)
    flow_t = jnp.transpose(flow, (1, 0, 2))
    adj_t = jnp.transpose(adjoint, (1, 0, 2))
    f32 = functools.partial(jax.ShapeDtypeStruct, dtype=jnp.float32)

    owner_t = jnp.transpose(lateral_owner, (1, 2, 0))
    link_t, ver_link_t = lateral_link.T, vertical_link.T
    i32 = functools.partial(jax.ShapeDtypeStruct, dtype=jnp.int32)
    requests, place = pl.pallas_call(
        functools.partial(plan_kernel, capacity),
        out_shape=(i32((peers, 1, LANES)), i32((blocks * 4,))),
        in_specs=[SMEM, SMEM],
        out_specs=(SMEM, SMEM),
        scratch_shapes=[pltpu.SMEM((peers,), jnp.int32)],
        name="plan",
    )(owner_t, link_t)

    received = (peers, capacity * 10, PLANE)
    returned, from_low, from_high = pl.pallas_call(
        functools.partial(halo_kernel, capacity),
        out_shape=(f32(received), f32((10, blocks, PLANE)), f32((10, blocks, PLANE))),
        in_specs=[VMEM] * 3,
        out_specs=(HBM, VMEM, VMEM),
        scratch_shapes=[
            pltpu.VMEM((4, 10, blocks, PLANE), jnp.float32),
            pltpu.VMEM((2, 10, blocks, PLANE), jnp.float32),
            pltpu.VMEM((peers, 1, LANES), jnp.int32),
            pltpu.SMEM((peers, 1, LANES), jnp.int32),
            pltpu.VMEM(received, jnp.float32),
            *[pltpu.SemaphoreType.DMA((peers,))] * 4,
            pltpu.SemaphoreType.DMA((2,)),
            pltpu.SemaphoreType.DMA((2,)),
            pltpu.SemaphoreType.DMA,
        ],
        compiler_params=pltpu.CompilerParams(collective_id=0, has_side_effects=True),
        name="halo",
    )(requests, flow_t, adj_t)

    tile = functools.partial(pltpu.VMEM, dtype=jnp.float32)
    return pl.pallas_call(
        main_kernel,
        out_shape=f32((blocks, EDGE * PLANE)),
        in_specs=[SMEM] * 3 + [VMEM] * 3 + [HBM] * 3,
        out_specs=VMEM,
        scratch_shapes=[
            tile(received),
            tile((10, blocks, PLANE)),
            tile((10, blocks, PLANE)),
            pltpu.SemaphoreType.DMA((3,)),
            tile((groups, 10, EDGE + 2, 8, LANES)),
            tile((3, 10, EDGE + 2, 8, LANES)),
            tile((groups, EDGE + 2, 8, LANES)),
            tile((groups, 6, 10, 8, LANES)),
            tile((4, 5, 8, LANES)),
            tile((4, 5, 8, LANES)),
            tile((15, 8, LANES)),
            tile((15, 8, LANES)),
            tile((15, 8, LANES)),
            tile((groups, EDGE, 8, LANES)),
        ],
        compiler_params=pltpu.CompilerParams(vmem_limit_bytes=50 * 1024 * 1024),
        name="indicator",
    )(
        place, link_t, ver_link_t,
        flow_t, adj_t, cut_flag, returned, from_low, from_high,
    )


def solution(mesh):
    spec3 = P(("blk", "grp"), None, None)
    spec2 = P(("blk", "grp"), None)
    return jax.shard_map(
        local,
        mesh=mesh,
        in_specs=(spec3, spec3, spec2, spec3, spec2, spec2),
        out_specs=spec2,
        check_vma=False,
    )
```

```python
import functools

import jax
import jax.numpy as jnp
from jax import lax
from jax.experimental import pallas as pl
from jax.experimental.pallas import tpu as pltpu
from jax.sharding import PartitionSpec as P

EDGE = 16
PLANE = EDGE * EDGE
LANES = 128
PACK = 4
FREESTREAM = (1.0, 0.0, 0.0, 0.3, 1.0)
VMEM = pl.BlockSpec(memory_space=pltpu.VMEM)
SMEM = pl.BlockSpec(memory_space=pltpu.SMEM)
HBM = pl.BlockSpec(memory_space=pltpu.HBM)
MESH = pl.DeviceIdType.MESH


def iota(shape, dim):
    return lax.broadcasted_iota(jnp.int32, shape, dim)


def primitive(state):
    density, mom, energy = state[0], state[1:4], state[4]
    root = lax.rsqrt(density)
    inverse = root * root
    vel = [m * inverse for m in mom]
    square = vel[0] * vel[0] + vel[1] * vel[1] + vel[2] * vel[2]
    return [density, *vel, 0.4 * (energy - 0.5 * density * square)]


def pack_cells(flow_ref, adj_ref, flag_ref, val_ref, solid_ref):
    blocks = flow_ref.shape[1]
    groups = blocks // PACK
    top = iota((8, LANES), 0) < PACK

    def pack(parts):
        tiles = []
        for g in range(groups):
            at = g * PACK % 8
            first, second = parts[g * PACK // 8]
            if first.shape[0] == PACK:
                tiles.append(jnp.concatenate([first, second], axis=0))
            elif at == 0:
                tiles.append(jnp.where(top, first, pltpu.roll(second, 4, 0)))
            else:
                tiles.append(jnp.where(top, pltpu.roll(first, 4, 0), second))
        return tiles

    def read(load, i):
        parts = []
        for start in range(0, blocks, 8):
            rows = slice(start, min(start + 8, blocks))
            parts.append(
                [load(rows, pl.ds(pl.multiple_of(i * PLANE + h * LANES, LANES), LANES)) for h in range(2)]
            )
        return pack(parts)

    def load_layer(i, carry):
        flow = [read(lambda r, s: flow_ref[c, r, s], i) for c in range(5)]
        for g in range(groups):
            for c, x in enumerate(primitive([f[g] for f in flow])):
                val_ref[g, c, i] = x
        for c in range(5):
            for g, x in enumerate(read(lambda r, s: adj_ref[c, r, s], i)):
                val_ref[g, 5 + c, i] = x
        for g, x in enumerate(read(lambda r, s: flag_ref[r, s], i)):
            solid_ref[g, i] = x.astype(jnp.float32)
        return carry

    lax.fori_loop(0, EDGE, load_layer, 0)


def halo_kernel(
    capacity, req_ref, flow_ref, adj_ref, flag_ref, ret_ref, low_ref, high_ref, val_hbm, solid_hbm,
    lat_ref, ver_ref, want_ref, index_ref, stage,
    ask_sem, asked_sem, send_sem, recv_sem, up_sem, down_sem, own_sem, val_ref, solid_ref, pack_sem,
):
    blocks = flow_ref.shape[1]
    peers = req_ref.shape[0]
    me = lax.axis_index("blk")

    def request(d):
        peer = lax.rem(me + d, peers)
        return pltpu.make_async_remote_copy(
            src_ref=req_ref.at[peer],
            dst_ref=want_ref.at[me],
            send_sem=ask_sem.at[d],
            recv_sem=asked_sem.at[d],
            device_id={"blk": peer},
            device_id_type=MESH,
        )

    barrier = pltpu.get_barrier_semaphore()
    for d in range(1, peers):
        pl.semaphore_signal(
            barrier, inc=1, device_id={"blk": lax.rem(me + d, peers)}, device_id_type=MESH
        )
    region = lax.axis_index("grp")
    last = lax.axis_size("grp") - 1
    has_low, has_high = region > 0, region < last
    for there, step in ((has_low, -1), (has_high, 1)):
        @pl.when(there)
        def _():
            pl.semaphore_signal(
                barrier, inc=1, device_id={"grp": region + step}, device_id_type=MESH
            )
    own = pltpu.make_async_copy(req_ref.at[me], want_ref.at[me], own_sem)
    own.start()
    lane = iota((blocks, LANES), 1)
    slot, spot = lane >> 4, lane & 15

    def layers(ref, c):
        def tile(i, half):
            return ref[c, :, i * PLANE + half * LANES : i * PLANE + (half + 1) * LANES]

        out = {}
        for half in range(2):
            out[0, half] = tile(0, half)
            out[1, half] = tile(EDGE - 1, half)
            low_j = high_j = low_k = high_k = jnp.zeros((blocks, LANES), jnp.float32)
            for i in range(EDGE):
                if i // 8 == half:
                    il = i % 8
                    low_j = jnp.where(slot == il, pltpu.roll(tile(i, 0), il * 16, 1), low_j)
                    high_j = jnp.where(
                        slot == il, pltpu.roll(tile(i, 1), (il * 16 + 16) % LANES, 1), high_j
                    )
                here = tile(i, half)
                low_k = jnp.where(spot == i, pltpu.roll(here, i, 1), low_k)
                high_k = jnp.where(spot == i, pltpu.roll(here, (LANES + i - 15) % LANES, 1), high_k)
            out[2, half], out[3, half], out[4, half], out[5, half] = low_j, high_j, low_k, high_k
        return out

    def put(face, half, c, value):
        where = slice(half * LANES, (half + 1) * LANES)
        if face < 4:
            lat_ref[face, c, :, where] = value
        else:
            ver_ref[face - 4, c, :, where] = value

    for c in range(5):
        if c == 3:
            pl.semaphore_wait(
                barrier, peers - 1 + has_low.astype(jnp.int32) + has_high.astype(jnp.int32)
            )
            for d in range(1, peers):
                request(d).start()
        for (face, half), value in layers(flow_ref, c).items():
            put(face, half, c, value)
        for (face, half), value in layers(adj_ref, c).items():
            put(face, half, 5 + c, value)
    for half in range(2):
        where = slice(half * LANES, (half + 1) * LANES)
        for ref, count in ((lat_ref, 4), (ver_ref, 2)):
            for face in range(count):
                prim = primitive([ref[face, c, :, where] for c in range(5)])
                for c in range(1, 5):
                    ref[face, c, :, where] = prim[c]
    own.wait()
    for d in range(1, peers):
        request(d).wait()
    indices = pltpu.make_async_copy(want_ref, index_ref, own_sem)
    indices.start()
    indices.wait()
    def copy(d):
        peer = lax.rem(me + d, peers)
        return pltpu.make_async_remote_copy(
            src_ref=stage.at[peer],
            dst_ref=ret_ref.at[me],
            send_sem=send_sem.at[d],
            recv_sem=recv_sem.at[d],
            device_id={"blk": peer},
            device_id_type=MESH,
        )

    def vertical(source, target, sem, step):
        return pltpu.make_async_remote_copy(
            src_ref=ver_ref.at[source],
            dst_ref=target,
            send_sem=sem.at[0],
            recv_sem=sem.at[1],
            device_id={"grp": region + step},
            device_id_type=MESH,
        )

    upward = vertical(1, low_ref, up_sem, 1)
    downward = vertical(0, high_ref, down_sem, -1)
    def gather(peer, ref, at):
        def one(s, carry):
            code = index_ref[peer, 0, s]
            face, block = code & 3, code >> 2
            for c in range(10):
                ref[at, pl.ds(s * 10 + c, 1), :] = lat_ref[face, c, pl.ds(block, 1), :]
            return carry

        lax.fori_loop(0, capacity, one, 0)

    def fill(d):
        peer = lax.rem(me + d, peers)
        gather(peer, stage, peer)

    fill(1)

    @pl.when(has_high)
    def _():
        upward.start()

    @pl.when(has_low)
    def _():
        downward.start()

    def send(d, carry):
        fill(d)
        copy(d - 1).start()
        return carry

    lax.fori_loop(2, peers, send, 0)
    gather(me, stage, me)
    copy(peers - 1).start()

    def far(ref):
        for c in range(10):
            ref[c] = jnp.full(ref.shape[1:], FREESTREAM[c] if c < 5 else 0.0, jnp.float32)

    mine = pltpu.make_async_copy(stage.at[me], ret_ref.at[me], own_sem)
    mine.start()
    pack_cells(flow_ref, adj_ref, flag_ref, val_ref, solid_ref)

    @pl.when(has_low)
    def _():
        downward.wait_send()
        upward.wait_recv()

    @pl.when(jnp.logical_not(has_low))
    def _():
        far(low_ref)

    @pl.when(has_high)
    def _():
        upward.wait_send()
        downward.wait_recv()

    @pl.when(jnp.logical_not(has_high))
    def _():
        far(high_ref)

    packed = [
        pltpu.make_async_copy(val_ref, val_hbm, pack_sem.at[0]),
        pltpu.make_async_copy(solid_ref, solid_hbm, pack_sem.at[1]),
    ]
    for copy_out in packed:
        copy_out.start()

    def finish(d, carry):
        copy(d).wait()
        return carry

    lax.fori_loop(1, peers, finish, 0)
    mine.wait()
    for copy_out in packed:
        copy_out.wait()


def plan_kernel(capacity, owner_ref, link_ref, req_ref, place_ref, count_ref):
    def clear(p, carry):
        count_ref[p] = 0
        for s in range(capacity):
            req_ref[p, 0, s] = 0
        return carry

    lax.fori_loop(0, req_ref.shape[0], clear, 0)

    def ask(b, carry):
        for f in range(4):
            owner = owner_ref[f, 0, b]
            at = count_ref[owner]
            count_ref[owner] = at + 1
            req_ref[owner, 0, at] = link_ref[f, b] // 5 * 4 + (f ^ 1)
            place_ref[b * 4 + f] = owner * 4096 + at
        return carry

    lax.fori_loop(0, link_ref.shape[1], ask, 0)


def minmod(a, b):
    return jnp.where(a * b > 0.0, jnp.where(jnp.abs(a) < jnp.abs(b), a, b), 0.0)


def derive(state):
    rho, u, v, w, p = state
    inv_root = lax.rsqrt(rho)
    root = rho * inv_root
    enth = (3.5 * p) * (inv_root * inv_root) + 0.5 * (u * u + v * v + w * w)
    return (rho, (u, v, w), p, enth, root, (root * u, root * v, root * w), root * enth)


def roe(left, right, n):
    rho_l, vel_l, p_l, h_l, root_l, rv_l, rh_l = left
    rho_r, vel_r, p_r, h_r, root_r, rv_r, rh_r = right
    t1, t2 = [a for a in range(3) if a != n]
    r = lax.rsqrt(root_l + root_r)
    inv = r * r
    vel = [(a + b) * inv for a, b in zip(rv_l, rv_r)]
    enth = (rh_l + rh_r) * inv
    half_sq = 0.5 * (vel[0] * vel[0] + vel[1] * vel[1] + vel[2] * vel[2])
    c_sq = 0.4 * (enth - half_sq)
    inv_c = lax.rsqrt(c_sq)
    c = c_sq * inv_c
    inv_c_sq = inv_c * inv_c
    rho = root_l * root_r
    un = vel[n]
    dp = p_r - p_l
    scaled = dp * inv_c_sq
    half = 0.5 * scaled
    jump = (0.5 * (rho * inv_c)) * (vel_r[n] - vel_l[n])
    spread, tenth, factor = 0.2 * c, 0.1 * c, 2.5 * inv_c

    def rate(x):
        x = jnp.abs(x)
        return jnp.where(x < spread, x * x * factor + tenth, x)

    slow = rate(un - c) * (half - jump)
    fast = rate(un + c) * (half + jump)
    speed = jnp.abs(un)
    mid = speed * ((rho_r - rho_l) - scaled)
    shear = speed * rho
    both = slow + fast
    diff = c * (fast - slow)
    mass = both + mid
    s1 = shear * (vel_r[t1] - vel_l[t1])
    s2 = shear * (vel_r[t2] - vel_l[t2])
    m_l, m_r = rho_l * vel_l[n], rho_r * vel_r[n]
    out = [None] * 5
    out[0] = m_l + m_r - mass
    out[1 + n] = m_l * vel_l[n] + m_r * vel_r[n] + (p_l + p_r) - (un * mass + diff)
    out[1 + t1] = m_l * vel_l[t1] + m_r * vel_r[t1] - (vel[t1] * mass + s1)
    out[1 + t2] = m_l * vel_l[t2] + m_r * vel_r[t2] - (vel[t2] * mass + s2)
    out[4] = (
        m_l * h_l + m_r * h_r
        - (enth * both + un * diff + mid * half_sq + vel[t1] * s1 + vel[t2] * s2)
    )
    return out


def quads(base, q1, q2):
    low = [b - q for b, q in zip(base, q1)]
    high = [b + q for b, q in zip(base, q1)]
    return [
        derive([b - q for b, q in zip(low, q2)]),
        derive([b + q for b, q in zip(low, q2)]),
        derive([b - q for b, q in zip(high, q2)]),
        derive([b + q for b, q in zip(high, q2)]),
    ]


def moments(lefts, rights, n):
    f = [roe(a, b, n) for a, b in zip(lefts, rights)]
    zero, first, second = [], [], []
    for c in range(5):
        low, high = f[0][c] + f[1][c], f[2][c] + f[3][c]
        zero.append(low + high)
        first.append(high - low)
        second.append((f[1][c] - f[0][c]) + (f[3][c] - f[2][c]))
    return zero + first + second


def dot(a, b):
    total = a[0] * b[0]
    for x, y in zip(a[1:], b[1:]):
        total = total + x * y
    return total


def main_kernel(
    place_ref, link_ref, ver_link_ref,
    ret_hbm, low_hbm, high_hbm, val_hbm, solid_hbm,
    out_ref,
    ret_ref, low_ref, high_ref, sems,
    val, slope, solid, ghost, low_k, low_j, mom_k, mom_j, mom_i, lo_solid,
):
    blocks = link_ref.shape[1]
    groups = blocks // PACK
    lane = iota((8, LANES), 1)
    row = iota((8, LANES), 0)
    top = row < PACK
    slot, spot = lane >> 4, lane & 15

    pairs = ((ret_hbm, ret_ref), (low_hbm, low_ref), (high_hbm, high_ref))
    copies = [pltpu.make_async_copy(a, b, sems.at[at]) for at, (a, b) in enumerate(pairs)]
    inside = pl.ds(1, EDGE)
    cells = [
        pltpu.make_async_copy(val_hbm, val.at[:, :, inside], sems.at[3]),
        pltpu.make_async_copy(solid_hbm, solid.at[:, inside], sems.at[4]),
    ]
    for copy in copies + cells:
        copy.start()
    for copy in copies:
        copy.wait()

    def load_ghost(c, carry):
        for b in range(blocks):
            g, at = b // PACK, b % PACK
            for f in range(6):
                if f < 4:
                    at_row = place_ref[b * 4 + f]
                    x = ret_ref[at_row >> 12, pl.ds((at_row & 4095) * 10 + c, 1), :]
                else:
                    ref = low_ref if f == 4 else high_ref
                    x = ref[c, pl.ds(ver_link_ref[f - 4, b] // 5, 1), :]
                ghost[g, f, c, at : at + 1, :] = x[:, :LANES]
                ghost[g, f, c, PACK + at : PACK + at + 1, :] = x[:, LANES:]
        return carry

    lax.fori_loop(0, 10, load_ghost, 0)
    upper_half = 1 - (row >> 2)
    for g in range(groups):
        for f in range(6):
            code = 0
            for at in range(PACK):
                b = g * PACK + at
                one = lax.rem(link_ref[f, b] if f < 4 else ver_link_ref[f - 4, b], 5)
                if f >= 4:
                    one = jnp.where(one == 4, 4, ((one & 1) << 1) + (one >> 1))
                code = jnp.where((row & 3) == at, one, code)
            half = 1 - upper_half
            own = (code == 4) | ((code >> 1) == half)
            quarter = ((4 * half + (slot >> 1)) << 4) + ((code & 1) << 3) + (spot >> 1)
            index = jnp.where(code == 4, lane, quarter)
            for c in range(10):
                x = ghost[g, f, c]
                x = jnp.where(own, x, pltpu.roll(x, 4, 0))
                x = jnp.take_along_axis(x, index, axis=1, mode="promise_in_bounds")
                ghost[g, f, c] = x
    for g in range(groups):
        nothing = jnp.zeros((8, LANES), jnp.float32)
        solid[g, 0] = nothing
        solid[g, EDGE + 1] = nothing
        for c in range(10):
            val[g, c, 0] = ghost[g, 0, c]
            val[g, c, EDGE + 1] = ghost[g, 1, c]
    for d in range(3):
        for c in range(5):
            nothing = jnp.zeros((8, LANES), jnp.float32)
            slope[d, c, 0] = nothing
            slope[d, c, EDGE + 1] = nothing

    for copy in cells:
        copy.wait()

    def next_k(x, edge, i):
        edge = 0.0 if edge is None else pltpu.roll(edge, 15 - i, 1)
        return jnp.where(spot == 15, edge, pltpu.roll(x, LANES - 1, 1))

    def prev_k(x, edge, i):
        edge = 0.0 if edge is None else pltpu.roll(edge, (LANES - i) % LANES, 1)
        return jnp.where(spot == 0, edge, pltpu.roll(x, 1, 1))

    def place(edge, i, lane_at, upper):
        if edge is None:
            return 0.0
        edge = pltpu.roll(edge, (2 * LANES + lane_at - (i & 7) * 16) % LANES, 1)
        same = (i >> 3) == (1 if upper else 0)
        return jnp.where(same, edge, pltpu.roll(edge, 4, 0))

    def next_j(x, edge, i):
        y = pltpu.roll(x, LANES - 16, 1)
        z = jnp.where(top, pltpu.roll(y, 4, 0), place(edge, i, LANES - 16, True))
        return jnp.where(slot == 7, z, y)

    def prev_j(x, edge, i):
        y = pltpu.roll(x, 16, 1)
        z = jnp.where(top, place(edge, i, 0, False), pltpu.roll(y, 4, 0))
        return jnp.where(slot == 0, z, y)

    def group(g, carry):
        def slopes(i, inner):
            at_k = spot == i
            at_j = ((row >> 2) == (i >> 3)) & (slot == (i & 7))
            for c in range(10):
                own = val[g, c, 1 + i]
                found = [
                    minmod(val[g, c, 2 + i] - own, own - val[g, c, i]),
                    minmod(next_j(own, ghost[g, 3, c], i) - own, own - prev_j(own, ghost[g, 2, c], i)),
                    minmod(next_k(own, ghost[g, 5, c], i) - own, own - prev_k(own, ghost[g, 4, c], i)),
                ]
                found = [0.25 * s for s in found]
                for d in range(3):
                    slope[d, c, 1 + i] = found[d]
                if c < 5:
                    for d, x in enumerate([own, *found]):
                        low_k[d, c] = jnp.where(at_k, pltpu.roll(x, i, 1), low_k[d, c])
                        x = jnp.where(top, x, pltpu.roll(x, 4, 0))
                        low_j[d, c] = jnp.where(at_j, pltpu.roll(x, (i & 7) * 16, 1), low_j[d, c])
            return inner

        lax.fori_loop(0, EDGE, slopes, 0)

        def first_faces(n, lower, cell):
            t1, t2 = [a for a in range(3) if a != n]
            left = derive(lower)
            base = [cell(0, c) - cell(1 + n, c) for c in range(5)]
            rights = quads(base, [cell(1 + t1, c) for c in range(5)], [cell(1 + t2, c) for c in range(5)])
            return moments([left] * 4, rights, n)

        for ref, n in ((mom_j, 1), (mom_k, 2)):
            source = low_j if n == 1 else low_k
            found = first_faces(n, [ghost[g, 2 * n, c] for c in range(5)], lambda d, c: source[d, c])
            for c in range(15):
                ref[c] = found[c]
        found = first_faces(
            0,
            [ghost[g, 0, c] for c in range(5)],
            lambda d, c: val[g, c, 1] if d == 0 else slope[d - 1, c, 1],
        )
        for c in range(15):
            mom_i[c] = found[c]

        def layer(i, inner):
            v = [val[g, c, 1 + i] for c in range(5)]
            q = [[slope[d, c, 1 + i] for c in range(5)] for d in range(3)]
            av = [val[g, 5 + c, 1 + i] for c in range(5)]
            aq = [[slope[d, 5 + c, 1 + i] for c in range(5)] for d in range(3)]
            child = {}
            for a in range(2):
                base = [x + y if a else x - y for x, y in zip(v, q[0])]
                for at, state in enumerate(quads(base, q[1], q[2])):
                    child[a, at >> 1, at & 1] = state

            def side(n, high):
                order = [(s, t) for s in range(2) for t in range(2)]
                return [child[tuple([*st[:n], high, *st[n:]])] for st in order]

            own_solid = solid[g, 1 + i]
            total = jnp.zeros((8, LANES), jnp.float32)
            for n in range(3):
                t1, t2 = [a for a in range(3) if a != n]
                f = [roe(a, b, n) for a, b in zip(side(n, 0), side(n, 1))]
                inside = [(f[0][c] + f[1][c]) + (f[2][c] + f[3][c]) for c in range(5)]
                total = total - 2.0 * dot(aq[n], inside)
                if n == 0:
                    base = [val[g, c, 2 + i] - slope[0, c, 2 + i] for c in range(5)]
                    q1 = [slope[1, c, 2 + i] for c in range(5)]
                    q2 = [slope[2, c, 2 + i] for c in range(5)]
                    up_solid, down_solid = solid[g, 2 + i], solid[g, i]
                else:
                    ahead, behind = (next_j, prev_j) if n == 1 else (next_k, prev_k)
                    base = [ahead(v[c] - q[n][c], ghost[g, 2 * n + 1, c], i) for c in range(5)]
                    q1 = [ahead(q[t1][c], None, i) for c in range(5)]
                    q2 = [ahead(q[t2][c], None, i) for c in range(5)]
                    up_solid, down_solid = ahead(own_solid, None, i), behind(own_solid, None, i)
                above = moments(side(n, 1), quads(base, q1, q2), n)
                if n == 0:
                    below = [mom_i[c] for c in range(15)]
                    for c in range(15):
                        mom_i[c] = above[c]
                else:
                    first = mom_j if n == 1 else mom_k
                    below = [behind(above[c], first[c], i) for c in range(15)]
                outer = [x + y for x, y in zip(av, aq[n])]
                inner_side = [x - y for x, y in zip(av, aq[n])]
                upper = dot([*outer, *aq[t1], *aq[t2]], above)
                lower = dot([*inner_side, *aq[t1], *aq[t2]], below)
                cross = aq[t1][1 + n] * q[t1][4] + aq[t2][1 + n] * q[t2][4]
                wall_up = 8.0 * (outer[1 + n] * (v[4] + q[n][4]) + cross)
                wall_down = 8.0 * (inner_side[1 + n] * (v[4] - q[n][4]) + cross)
                total = total + (
                    jnp.where(up_solid > 0.5, wall_up, upper)
                    - jnp.where(down_solid > 0.5, wall_down, lower)
                )
            total = jnp.where(own_solid > 0.5, 0.0, 0.5 * jnp.abs(total))
            lo_solid[g, i] = total
            return inner

        lax.fori_loop(0, EDGE, layer, 0)
        return carry

    lax.fori_loop(0, groups, group, 0)

    def store(i, carry):
        for g in range(groups):
            x = lo_solid[g, i]
            for h in range(2):
                out_ref[
                    g * PACK : (g + 1) * PACK,
                    pl.ds(pl.multiple_of(i * PLANE + h * LANES, LANES), LANES),
                ] = x[h * PACK : (h + 1) * PACK]
        return carry

    lax.fori_loop(0, EDGE, store, 0)


def local(flow, adjoint, cut_flag, lateral_owner, lateral_link, vertical_link):
    blocks = flow.shape[0]
    groups = blocks // PACK
    peers = lax.axis_size("blk")
    capacity = max(2, 6 * blocks // peers)
    flow_t = jnp.transpose(flow, (1, 0, 2))
    adj_t = jnp.transpose(adjoint, (1, 0, 2))
    f32 = functools.partial(jax.ShapeDtypeStruct, dtype=jnp.float32)

    owner_t = jnp.transpose(lateral_owner, (1, 2, 0))
    link_t, ver_link_t = lateral_link.T, vertical_link.T
    i32 = functools.partial(jax.ShapeDtypeStruct, dtype=jnp.int32)
    requests, place = pl.pallas_call(
        functools.partial(plan_kernel, capacity),
        out_shape=(i32((peers, 1, LANES)), i32((blocks * 4,))),
        in_specs=[SMEM, SMEM],
        out_specs=(SMEM, SMEM),
        scratch_shapes=[pltpu.SMEM((peers,), jnp.int32)],
        name="plan",
    )(owner_t, link_t)

    received = (peers, capacity * 10, PLANE)
    cells = (groups, 10, EDGE, 8, LANES)
    flags = (groups, EDGE, 8, LANES)
    returned, from_low, from_high, packed, solid = pl.pallas_call(
        functools.partial(halo_kernel, capacity),
        out_shape=(
            f32(received),
            f32((10, blocks, PLANE)),
            f32((10, blocks, PLANE)),
            f32(cells),
            f32(flags),
        ),
        in_specs=[VMEM] * 4,
        out_specs=(HBM, VMEM, VMEM, HBM, HBM),
        scratch_shapes=[
            pltpu.VMEM((4, 10, blocks, PLANE), jnp.float32),
            pltpu.VMEM((2, 10, blocks, PLANE), jnp.float32),
            pltpu.VMEM((peers, 1, LANES), jnp.int32),
            pltpu.SMEM((peers, 1, LANES), jnp.int32),
            pltpu.VMEM(received, jnp.float32),
            *[pltpu.SemaphoreType.DMA((peers,))] * 4,
            pltpu.SemaphoreType.DMA((2,)),
            pltpu.SemaphoreType.DMA((2,)),
            pltpu.SemaphoreType.DMA,
            pltpu.VMEM(cells, jnp.float32),
            pltpu.VMEM(flags, jnp.float32),
            pltpu.SemaphoreType.DMA((2,)),
        ],
        compiler_params=pltpu.CompilerParams(collective_id=0, has_side_effects=True),
        name="halo",
    )(requests, flow_t, adj_t, cut_flag)

    tile = functools.partial(pltpu.VMEM, dtype=jnp.float32)
    return pl.pallas_call(
        main_kernel,
        out_shape=f32((blocks, EDGE * PLANE)),
        in_specs=[SMEM] * 3 + [HBM] * 5,
        out_specs=VMEM,
        scratch_shapes=[
            tile(received),
            tile((10, blocks, PLANE)),
            tile((10, blocks, PLANE)),
            pltpu.SemaphoreType.DMA((5,)),
            tile((groups, 10, EDGE + 2, 8, LANES)),
            tile((3, 10, EDGE + 2, 8, LANES)),
            tile((groups, EDGE + 2, 8, LANES)),
            tile((groups, 6, 10, 8, LANES)),
            tile((4, 5, 8, LANES)),
            tile((4, 5, 8, LANES)),
            tile((15, 8, LANES)),
            tile((15, 8, LANES)),
            tile((15, 8, LANES)),
            tile((groups, EDGE, 8, LANES)),
        ],
        compiler_params=pltpu.CompilerParams(vmem_limit_bytes=63 * 1024 * 1024),
        name="indicator",
    )(
        place, link_t, ver_link_t,
        returned, from_low, from_high, packed, solid,
    )


def solution(mesh):
    spec3 = P(("blk", "grp"), None, None)
    spec2 = P(("blk", "grp"), None)
    return jax.shard_map(
        local,
        mesh=mesh,
        in_specs=(spec3, spec3, spec2, spec3, spec2, spec2),
        out_specs=spec2,
        check_vma=False,
    )
```
